32 devices in a mesh: own: 8 (over z, y), rep: 4 (over x, core).
Axes of the slice: x: 2, y: 2, z: 4, core: 2. Of those that a mesh axis runs over, the one named last changes fastest.
Arguments:
- hidden: bfloat16 [1024, 1024], P('own', 'rep'), may hold values from -140 to 140
- weight: bfloat16 [8, 2048, 1024], P('own', None, 'rep'), may hold values from -0.1875 to 0.1875
- bucket_map: int32 [8], replicated, may hold values from 0 to 7, each once
- active: int32 [1024, 2], P('own'), may hold values from 0 to 7, all different within a row; in each aligned block of 128 rows (0 to 127, 128 to 255, ...) at most 64 rows name the same one
- label_pick: int32 [1024], P('own'), may hold values from 0 to 4095
Outputs:
- sample_loss: float32 [1024], P('own')
- grad_hidden: float32 [1024, 1024], P('own', 'rep')
- grad_weight: bfloat16 [8, 2048, 1024], P('own', None, 'rep')
The draws below stay inside these ranges and needn't reach their ends.
Inputs may be any that keep to these rules, and one draw needn't show every extreme that they name: `bucket_map`: each weight slot is named once. `active`: A sample's 2 bucket ids differ. Among the 128 samples of one index of own, no bucket is named by more than 64 samples, a bound that some block reaches.
All inputs are finite; a program needn't handle non-finite values.
Results may differ from the reference program's by a relative error of at most 0.0032.
Values may be sent and summed in bfloat16 or wider, within the bound.
A program may use at most 64 MiB of HBM per device.

```python
import math
import jax
import jax.numpy as jnp
import numpy as np
from jax import lax

D = 1024
LB = 2048
K = 2
SAMP_DEV = 128
BUCKETS = 8
SAMPLES = 1024
MOST = 64
CAP_BUCKET = 512


def draw_hidden(key, part):
    first_key = jax.random.fold_in(key, 0)
    return (3.0 * jax.random.truncated_normal(first_key, -6.0, 6.0, (SAMPLES, D), jnp.float32)).astype(jnp.bfloat16)


def place_ends(drawn, rng, least, largest):
    dims = drawn.shape
    index_at = [jax.random.randint(jax.random.fold_in(rng, axis), (), 0, dims[axis]) for axis in range(len(dims))]
    drawn = drawn.at[tuple(index_at)].set(least)
    longest = dims.index(max(dims))
    index_at[longest] = (index_at[longest] + 1) % dims[longest]
    return drawn.at[tuple(index_at)].set(largest)


def shard_levels(rng, shape, shards, least, high):
    def one(position, parts):
        draws = jax.random.uniform(jax.random.fold_in(jax.random.fold_in(rng, 6), position), (parts,), jnp.float32, least / len(shards), high / len(shards))
        return jnp.repeat(jnp.exp(draws), shape[position] // parts).reshape((-1,) + (1,) * (len(shape) - position - 1))

    loudness = one(*shards[0])
    for cut in shards[1:]:
        loudness = loudness * one(*cut)
    return loudness


def routed_block(rng, own, number, rows, count, top, most, skew):
    order = jax.random.permutation(rng, count)
    heavy_load, usual = shares(count, rows * top, most, skew, True), shares(count, rows * top, most, skew, False)
    places = jnp.arange(count)

    def named(lengths, rotation):
        used = int((lengths > 0).sum())
        fixed = max(1, used // 4)
        passed = fixed + (places - fixed + rotation * (used - fixed)) % max(1, count - fixed)
        return jnp.zeros((count,), jnp.int32).at[order[jnp.where(places < fixed, places, passed)]].set(jnp.asarray(lengths, jnp.int32))

    lengths = jnp.where(number % 4 == 0, named(heavy_load, number // 4), named(usual, number - number // 4 - 1))
    mixed = jax.random.permutation(jax.random.fold_in(own, 3), count)
    donor, receiver = mixed[0:count // 2 * 2:2], mixed[1:count // 2 * 2:2]
    slack = jnp.minimum(lengths[donor] - 1, most - lengths[receiver]) // 2
    slack = jnp.where((donor == order[0]) | (receiver == order[0]) | (lengths[receiver] == 0), 0, jnp.maximum(slack, 0))
    passed = jax.random.randint(jax.random.fold_in(own, 4), (count // 2,), 0, 1 << 20) % (slack + 1)
    lengths = lengths.at[donor].add(-passed).at[receiver].add(passed)
    labels = jnp.searchsorted(jnp.cumsum(lengths), jnp.arange(rows * top), side="right").astype(jnp.int32)
    listing = labels.reshape(top, rows).T
    listing = listing[jax.random.permutation(jax.random.fold_in(own, 1), rows)]
    rotation = jax.random.randint(jax.random.fold_in(own, 2), (rows, 1), 0, top)
    return jnp.take_along_axis(listing, (jnp.arange(top)[None, :] + rotation) % top, axis=1)


def shares(amount, total, limit, skew, full):
    loads = [(1 << 20) // math.isqrt(grade ** skew) + 1 for grade in range(1, amount + 1)]
    largest = limit if full else min(limit, max(-(-total // amount), total * loads[0] // sum(loads)))
    least = 1 if total - largest >= amount - 1 else 0
    given, surplus = [largest] + [least] * (amount - 1), total - largest - least * (amount - 1)
    while surplus > 0:
        candidates = [i for i in range(1, amount) if given[i] < largest] or [i for i in range(1, amount) if given[i] < limit]
        whole, remaining = sum([loads[i] for i in candidates]), surplus
        for i in candidates:
            addition = min(limit - given[i], max(1, remaining * loads[i] // whole), surplus)
            given[i] = given[i] + addition
            surplus = surplus - addition
    return np.array(given)


def bell_draw(own_key, shape, width, limit, cuts=(), kind=jnp.bfloat16):
    array = jax.random.normal(own_key, shape, jnp.float32) * width
    if len(cuts) > 0:
        array = shard_levels(own_key, shape, cuts, -0.22, 0.18) * array
    return jnp.clip(array, min=-limit, max=limit).astype(kind)


def setup_inputs(seed: int = 0) -> dict:
    keys = jax.random.split(jax.random.key(seed), 6)
    hidden = draw_hidden(jax.random.fold_in(keys[5], 71), 0)
    weight = bell_draw(keys[1], (BUCKETS, LB, D), D ** -0.5, 0.1875, ((0, 8), (2, 4)))
    bucket_map = jax.random.permutation(keys[2], BUCKETS).astype(jnp.int32)
    active_keys = jax.random.split(jax.random.fold_in(keys[3], 1), SAMPLES // SAMP_DEV)
    active_turns = jax.random.permutation(jax.random.fold_in(keys[3], 3), SAMPLES // SAMP_DEV)
    active = jax.vmap(lambda own, number: routed_block(jax.random.fold_in(keys[3], 2), own, number, SAMP_DEV, BUCKETS, K, MOST, 2))(active_keys, active_turns).reshape((SAMPLES, K))
    label_pick = place_ends(jax.random.randint(keys[4], (SAMPLES,), 0, K * LB), jax.random.fold_in(keys[4], 1), 0, (K * LB) - 1).astype(jnp.int32)
    return {"hidden": hidden, "weight": weight, "bucket_map": bucket_map, "active": active, "label_pick": label_pick}


def reference(hidden, weight, bucket_map, active, label_pick):
    pair_count = SAMPLES * K
    slot_index = bucket_map[active].reshape(pair_count).astype(jnp.int32)
    pair_index = jnp.arange(pair_count, dtype=jnp.int32)
    sample_of = pair_index // K
    pick_value = label_pick[sample_of]
    target_col = jnp.where(pick_value // LB == pair_index % K, pick_value % LB, -1).astype(jnp.int32)
    order_pairs = jnp.argsort(slot_index, stable=True).astype(jnp.int32)
    counts = jax.ops.segment_sum(jnp.ones((pair_count,), jnp.int32), slot_index, BUCKETS)
    starts = (jnp.cumsum(counts) - counts).astype(jnp.int32)
    order_padded = jnp.concatenate([order_pairs, jnp.zeros((CAP_BUCKET,), jnp.int32)])
    columns = jnp.arange(LB, dtype=jnp.int32)[None, :]
    local_rows = jnp.arange(CAP_BUCKET, dtype=jnp.int32)

    def rows_of(bucket):
        picked = lax.dynamic_slice(order_padded, (starts[bucket],), (CAP_BUCKET,)).astype(jnp.int32)
        valid = local_rows < counts[bucket]
        gathered = jnp.where(valid[:, None], hidden[sample_of[picked]], jnp.zeros((), jnp.bfloat16))
        logits = jnp.dot(gathered, weight[bucket].T, preferred_element_type=jnp.float32)
        return picked, valid, gathered, logits

    def stats_of(bucket):
        picked, valid, gathered, logits = rows_of(bucket)
        row_max = jnp.max(logits, axis=1)
        row_sum = jnp.sum(jnp.exp(logits - row_max[:, None]), axis=1)
        row_target = jnp.sum(jnp.where(columns == target_col[picked][:, None], logits, 0.0), axis=1)
        dest = jnp.where(valid, picked, pair_count)
        return dest, row_max, row_sum, row_target

    dest, row_max, row_sum, row_target = lax.map(stats_of, jnp.arange(BUCKETS, dtype=jnp.int32))
    dest = dest.reshape(-1)
    pair_max = jnp.zeros((pair_count,), jnp.float32).at[dest].set(row_max.reshape(-1), mode="drop")
    pair_sum = jnp.zeros((pair_count,), jnp.float32).at[dest].set(row_sum.reshape(-1), mode="drop")
    pair_target = jnp.zeros((pair_count,), jnp.float32).at[dest].set(row_target.reshape(-1), mode="drop")
    pair_max = pair_max.reshape(SAMPLES, K)
    peak_max = jnp.max(pair_max, axis=1)
    norm_sum = jnp.sum(pair_sum.reshape(SAMPLES, K) * jnp.exp(pair_max - peak_max[:, None]), axis=1)
    log_norm = peak_max + jnp.log(norm_sum)
    sample_loss = log_norm - jnp.sum(pair_target.reshape(SAMPLES, K), axis=1)
    pair_norm = jnp.repeat(log_norm, K)

    def grads_of(carry, bucket):
        picked, valid, gathered, logits = rows_of(bucket)
        onehot = (columns == target_col[picked][:, None]).astype(jnp.float32)
        grad_logits = jnp.exp(logits - pair_norm[picked][:, None]) - onehot
        grad_logits = jnp.where(valid[:, None], grad_logits, 0.0).astype(jnp.bfloat16)
        block_grad = jnp.dot(grad_logits.T, gathered, preferred_element_type=jnp.float32).astype(jnp.bfloat16)
        row_grads = jnp.dot(grad_logits, weight[bucket], preferred_element_type=jnp.float32)
        sample_dest = jnp.where(valid, sample_of[picked], SAMPLES)
        carry = carry.at[sample_dest].add(row_grads, mode="drop")
        return carry, block_grad

    grad_hidden, grad_weight = lax.scan(grads_of, jnp.zeros((SAMPLES, D), jnp.float32), jnp.arange(BUCKETS, dtype=jnp.int32))
    return sample_loss, grad_hidden, grad_weight
```

```python
import functools
import jax
import jax.numpy as jnp
from jax import lax
from jax.experimental import pallas as pl
from jax.experimental.pallas import tpu as pltpu
from jax.sharding import PartitionSpec as P

MESH = pl.DeviceIdType.MESH
F32 = jnp.float32
BF16 = jnp.bfloat16
NT = (((1,), (1,)), ((), ()))
TN = (((0,), (0,)), ((), ()))


def ranks(slot0, slot1, buckets, upper):
    sources, samples = slot0.shape
    bucket = lax.broadcasted_iota(jnp.int32, (buckets, samples), 0)
    hits = [
        jnp.where((slot0[s : s + 1] == bucket) | (slot1[s : s + 1] == bucket), 1.0, 0.0)
        for s in range(sources)
    ]
    hits = jnp.concatenate(hits, axis=0) if sources > 1 else hits[0]
    earlier = jnp.dot(hits.astype(BF16), upper, preferred_element_type=F32)
    return jnp.where(hits > 0.5, earlier, -1.0).astype(jnp.int32)


def lane_pick(values, index):
    return jnp.take_along_axis(values, index, axis=1)


def kernel(
    n, depth, act_hbm, pick_hbm, map_hbm, hidden_hbm, weight_hbm,
    loss_ref, gh_ref, gw_ref,
    act, pick_own, table_in, meta, hidden, hidden_x, weight, metas, wfull, sendbuf, sendbuf_x, rows, stats, statrep, comb, statown,
    norms, tsums, row_target, row_valid, row_norm, e_all, g_all, gw_acc, ghsend, ghrecv,
    s_loc, s_hx, r_hx, s_meta, r_meta, s_w, r_w, s_row, r_row, s_rowx, r_rowx, s_fc, r_fc, s_fr, r_fr,
    s_sr, r_sr, s_so, r_so, s_gx, r_gx, s_gc, r_gc, s_gr, r_gr, s_gh, r_gh,
):
    labels, part = weight_hbm.shape
    samples = hidden_hbm.shape[0]
    cols = labels // 4
    pairs = n // 2
    o = lax.axis_index("own")
    r = lax.axis_index("rep")
    z = o // 2
    y = o - 2 * z
    p1 = r + 1 - 2 * lax.rem(r, 2)
    p2 = lax.rem(r + 2, 4)
    p3 = lax.rem(p1 + 2, 4)
    row_count = n * depth
    local = [
        pltpu.make_async_copy(act_hbm, act, s_loc.at[0]),
        pltpu.make_async_copy(hidden_hbm, hidden, s_loc.at[1]),
        pltpu.make_async_copy(weight_hbm, weight, s_loc.at[2]),
        pltpu.make_async_copy(
            weight_hbm.at[pl.ds(pl.multiple_of(r * cols, cols), cols)],
            wfull.at[:, pl.ds(pl.multiple_of(r * part, part), part)],
            s_loc.at[3],
        ),
        pltpu.make_async_copy(pick_hbm, pick_own, s_loc.at[4]),
        pltpu.make_async_copy(map_hbm, table_in, s_loc.at[5]),
    ]

    def send(src, dst, ssem, rsem, own, rep):
        copy = pltpu.make_async_remote_copy(
            src_ref=src, dst_ref=dst, send_sem=ssem, recv_sem=rsem,
            device_id={"own": own, "rep": rep}, device_id_type=MESH,
        )
        copy.start()

    def wait(ref, sem):
        pltpu.make_async_copy(ref, ref, sem).wait()

    def peer(k):
        return lax.rem(o + k, n)

    def at_rows(s):
        return pl.ds(pl.multiple_of(s * depth, depth), depth)

    def spot(source, owner):
        turn = lax.rem(source // 2 - owner // 2 + pairs + pairs - 1, pairs)
        return at_rows(2 * turn + lax.rem(source, 2))

    def pair_at(p):
        return lax.rem(z + 1 + p, pairs)

    def at_part(q):
        return pl.ds(pl.multiple_of(q * part, part), part)

    unit = cols // 4
    pieces = ((0, cols - unit), (cols - unit, unit))

    def at_cols(q, start=0, size=None):
        size = cols if size is None else size
        return pl.ds(pl.multiple_of(q * cols + start, unit), size)

    def lanes(p):
        return slice(p * 2 * depth, (p + 1) * 2 * depth)

    barrier = pltpu.get_barrier_semaphore()
    for k in range(1, n):
        pl.semaphore_signal(barrier, inc=1, device_id={"own": peer(k), "rep": r}, device_id_type=MESH)
    for q in (p1, p2, p3):
        pl.semaphore_signal(barrier, inc=1, device_id={"own": o, "rep": q}, device_id_type=MESH)
    for c in local:
        c.start()
    local[0].wait()
    local[4].wait()
    local[5].wait()
    meta[0:2, :] = act[...]
    meta[2:3, :] = pick_own[...]
    meta[3:8, :] = jnp.zeros((5, samples), jnp.int32)
    meta[3:4, 0:n] = table_in[...]
    local[1].wait()
    below = lax.broadcasted_iota(jnp.int32, (samples, samples), 0)
    right = lax.broadcasted_iota(jnp.int32, (samples, samples), 1)
    upper = jnp.where(below < right, 1.0, 0.0).astype(BF16)

    def slots(ids):
        table = jnp.broadcast_to(meta[3:4, :], (n, samples))
        return lane_pick(table, jnp.broadcast_to(ids, (n, samples)))[: ids.shape[0]]

    mine = meta[...]
    own_rank = ranks(slots(mine[0:1]), slots(mine[1:2]), n, upper)
    place = lax.broadcasted_iota(jnp.int32, (depth, samples), 0)
    pack = jnp.concatenate(
        [jnp.where(own_rank[b : b + 1] == place, 1.0, 0.0).astype(BF16) for b in range(n)], axis=0
    )
    packed = jnp.dot(pack, hidden[...], preferred_element_type=F32).astype(BF16)
    for b in range(n):
        sendbuf[b] = packed[b * depth : (b + 1) * depth]
    pl.semaphore_wait(barrier, n - 1 + 3)
    send(hidden_hbm, hidden_x, s_hx, r_hx, o, p2)
    for k in range(1, n):
        send(meta, metas.at[o], s_meta, r_meta, peer(k), r)
    for k in range(1, n):
        send(sendbuf.at[peer(k)], rows.at[spot(o, peer(k)), at_part(r)], s_row, r_row, peer(k), r)
    for j, (start, size) in enumerate(pieces):
        for q in (p2, p3, p1):
            send(weight_hbm.at[at_cols(q, start, size)], wfull.at[start : start + size, at_part(r)], s_w, r_w.at[j], o, q)
    rows[spot(o, o), at_part(r)] = sendbuf[o]
    metas[o] = mine

    wait(hidden_x, r_hx)
    packed_x = jnp.dot(pack, hidden_x[...], preferred_element_type=F32).astype(BF16)
    for b in range(n):
        sendbuf_x[b] = packed_x[b * depth : (b + 1) * depth]
    for k in range(1, n):
        send(
            sendbuf_x.at[peer(k)], rows.at[spot(o, peer(k)), at_part(p2)], s_rowx, r_rowx.at[k - 1], peer(k), r
        )
    rows[spot(o, o), at_part(p2)] = sendbuf_x[o]

    wait(metas.at[0 : n - 1], r_meta)
    slot0 = slots(metas[:, 0, :])
    slot1 = slots(metas[:, 1, :])
    pick = metas[:, 2, :]
    rank_all = ranks(slot0, slot1, n, upper)
    wanted = jnp.where(pick < labels, slot0, slot1)
    code = jnp.where(wanted == o, jnp.where(pick < labels, pick, pick - labels) + 1, 0)
    code_hi = (code // 64).astype(F32)
    code_lo = (code - (code // 64) * 64).astype(F32)
    lane = lax.broadcasted_iota(jnp.int32, (1, samples), 1)
    sub = lax.broadcasted_iota(jnp.int32, (8, samples), 0)
    bucket_sub = lax.broadcasted_iota(jnp.int32, (n, samples), 0)
    row_index = []
    place2 = lax.broadcasted_iota(jnp.int32, (2 * depth, samples), 0)
    for sp in range(pairs):
        info = jnp.zeros((8, 2 * depth), F32)
        for h in range(2):
            s = 2 * sp + h
            rank_me = jnp.max(
                jnp.where(bucket_sub == o, rank_all[s * n : (s + 1) * n], -1), axis=0, keepdims=True
            )
            member = jnp.where(
                (rank_me >= 0) & (rank_me + h * depth == place2), 1.0, 0.0
            ).astype(BF16)
            facts = jnp.where(
                sub == 0, lane.astype(F32),
                jnp.where(sub == 1, code_hi[s : s + 1], jnp.where(sub == 2, code_lo[s : s + 1], jnp.where(sub == 3, 1.0, 0.0))),
            ).astype(BF16)
            info = info + lax.dot_general(facts, member, NT, preferred_element_type=F32)
        row_index.append(info[0:1].astype(jnp.int32))
        row_valid[sp : sp + 1, :] = info[3:4]
        row_target[sp : sp + 1, :] = (info[1:2] * 64.0 + info[2:3]).astype(jnp.int32) - 1
    targets_at = [row_target[pl.ds(pair_at(p), 1), :] for p in range(pairs)]
    target_row = jnp.concatenate(targets_at, axis=1)

    wait(rows.at[0 : (n - 1) * depth, 0:part], r_row)
    send(rows.at[:, at_part(r)], rows.at[:, at_part(r)], s_fc, r_fc, o, p1)
    for k in range(n):
        s = lax.rem(o - k + n, n)
        block = rows.at[spot(s, o), at_part(p2)]
        if k > 0:
            wait(block, r_rowx.at[k - 1])
        send(block, block, s_fr, r_fr, o, p1)
    local[2].wait()
    local[3].wait()
    wait(rows.at[:, 0:part], r_fc)
    wait(rows.at[:, 0:part], r_fr)

    def pass_x(p, start=0, size=None):
        block = e_all.at[p, at_cols(r, start, size), :]
        send(block, block, s_gx, r_gx.at[p], o, p2)

    def pass_c(start, size):
        block = e_all.at[:, at_cols(r, start, size), :]
        send(block, block, s_gc, r_gc, o, p1)

    tops, sums, targets = [], [], []
    for j, (start, size) in enumerate(pieces):
        wait(wfull.at[start : start + size, 0 : 3 * part], r_w.at[j])
        spans = ((0, 1), (1, pairs)) if j == 0 else ((0, pairs),)
        top_j, sum_j, target_j = [], [], []
        for first, last in spans:
            at = slice(first * 2 * depth, last * 2 * depth)
            width = (last - first) * 2 * depth
            logits = lax.dot_general(wfull[start : start + size, :], rows[at, :], NT, preferred_element_type=F32)
            top = jnp.max(logits, axis=0, keepdims=True)
            raised = jnp.exp(logits - top)
            for p in range(first, last):
                e_all[p, at_cols(r, start, size), :] = raised[:, (p - first) * 2 * depth : (p - first + 1) * 2 * depth].astype(BF16)
            if first == 0 and j == 0:
                pass_x(0, start, size)
            label_id = lax.broadcasted_iota(jnp.int32, (size, width), 0) + (r * cols + start)
            target_j.append(jnp.sum(jnp.where(label_id == target_row[:, at], logits, 0.0), axis=0, keepdims=True))
            sum_j.append(jnp.sum(raised, axis=0, keepdims=True))
            top_j.append(top)
        if j == 0:
            pass_c(start, size)
        targets.append(jnp.concatenate(target_j, axis=1))
        sums.append(jnp.concatenate(sum_j, axis=1))
        tops.append(jnp.concatenate(top_j, axis=1))
    target_sum = targets[0] + targets[1]
    peak = jnp.maximum(tops[0], tops[1])
    lse = peak + jnp.log(sums[0] * jnp.exp(tops[0] - peak) + sums[1] * jnp.exp(tops[1] - peak))
    for p in range(pairs):
        stats[p : p + 1, :] = lse[:, lanes(p)]
        stats[pairs + p : pairs + p + 1, :] = target_sum[:, lanes(p)]
        stats[n + p : n + p + 1, :] = tops[0][:, lanes(p)]
        stats[n + pairs + p : n + pairs + p + 1, :] = tops[1][:, lanes(p)]
    for q in (p2, p3, p1):
        send(stats, statrep.at[r], s_sr, r_sr, o, q)
    pass_x(0, *pieces[1])
    for p in range(1, pairs):
        pass_x(p)
    pass_c(*pieces[1])
    statrep[r] = stats[...]
    wait(statrep.at[0:3], r_sr)
    parts = [statrep[q, 0:n, :] for q in range(4)]
    high = jnp.maximum(jnp.maximum(parts[0], parts[1]), jnp.maximum(parts[2], parts[3]))
    total = high + jnp.log(sum(jnp.exp(x - high) for x in parts))
    summed = sum(parts)
    for p in range(pairs):
        comb[pl.ds(pair_at(p), 1), :] = total[p : p + 1]
        comb[pl.ds(pairs + pair_at(p), 1), :] = summed[pairs + p : pairs + p + 1]
    for k in range(1, n):
        send(comb, statown.at[o], s_so, r_so, peer(k), r)
    statown[o] = comb[...]

    def forward(p):
        block = e_all.at[p, at_cols(p2), :]
        wait(block, r_gx.at[p])
        send(block, block, s_gr, r_gr.at[p], o, p1)

    wait(e_all.at[:, at_cols(p1), :], r_gc)
    forward(0)
    forward(1)
    wait(statown.at[0 : n - 1], r_so)
    for sp in range(pairs):
        held = statown[:, sp, :]
        pair = []
        for h in range(2):
            s = 2 * sp + h
            rank = rank_all[s * n : (s + 1) * n]
            index = jnp.where(rank >= 0, rank + h * depth, 0)
            value = jnp.where(rank >= 0, lane_pick(held, index), -3.0e38)
            most = jnp.max(value, axis=0, keepdims=True)
            norm = most + jnp.log(jnp.sum(jnp.exp(value - most), axis=0, keepdims=True))
            norms[s : s + 1, :] = norm
            pair.append(
                lane_pick(jnp.broadcast_to(norm, (8, samples)), jnp.broadcast_to(row_index[sp], (8, samples)))[0:1]
            )
        row_norm[sp : sp + 1, :] = jnp.where(lane < depth, pair[0], pair[1])
    valid_at = [row_valid[pl.ds(pair_at(p), 1), :] > 0.5 for p in range(pairs)]
    norm_at = [row_norm[pl.ds(pair_at(p), 1), :] for p in range(pairs)]

    def term(p, q):
        for j, (start, size) in enumerate(pieces):
            at = at_cols(q, start, size)
            base = n + j * pairs + p
            high = statrep[pl.ds(q, 1), base : base + 1, :].reshape(1, samples)
            scale = jnp.where(valid_at[p], jnp.exp(high - norm_at[p]), 0.0)
            ids = lax.broadcasted_iota(jnp.int32, (size, samples), 0) + (q * cols + start)
            grad = e_all[p, at, :].astype(F32) * scale - jnp.where(ids == targets_at[p], 1.0, 0.0)
            g_all[at, lanes(p)] = grad.astype(BF16)
        at = at_cols(q)
        return lax.dot_general(g_all[at, lanes(p)], weight[at, :], TN, preferred_element_type=F32)

    def give_back(p):
        if p < pairs - 1:
            for h in range(2):
                at = slice((2 * p + h) * depth, (2 * p + h + 1) * depth)
                send(ghsend.at[at], ghrecv.at[at_rows(o)], s_gh, r_gh, 2 * pair_at(p) + h, r)
        else:
            send(ghsend.at[at_rows(2 * p + 1 - y)], ghrecv.at[at_rows(o)], s_gh, r_gh, 2 * z + 1 - y, r)
            ghrecv[at_rows(o), :] = ghsend[at_rows(2 * p + y), :]

    def block_of(p):
        return e_all.at[p, at_cols(p3), :]

    for p in range(2):
        acc = term(p, r) + term(p, p1) + term(p, p2)
        wait(block_of(p), r_gr.at[p])
        ghsend[lanes(p), :] = (acc + term(p, p3)).astype(BF16)
        give_back(p)
    acc2 = term(2, r) + term(2, p1)
    forward(2)
    acc2 = acc2 + term(2, p2)
    wait(block_of(2), r_gr.at[2])
    ghsend[lanes(2), :] = (acc2 + term(2, p3)).astype(BF16)
    give_back(2)
    acc3 = term(3, r) + term(3, p1)
    half = row_count // 2
    for c in range(4):
        at = slice(c * cols, (c + 1) * cols)
        gw_acc[at, :] = jnp.dot(g_all[at, 0:half], rows[0:half, at_part(r)], preferred_element_type=F32)
    for sp in range(pairs):
        held = statown[:, pairs + sp, :]
        for h in range(2):
            s = 2 * sp + h
            rank = rank_all[s * n : (s + 1) * n]
            index = jnp.where(rank >= 0, rank + h * depth, 0)
            value = jnp.where(rank >= 0, lane_pick(held, index), 0.0)
            tsums[s : s + 1, :] = jnp.sum(value, axis=0, keepdims=True)
    loss_ref[...] = norms[pl.ds(o, 1), :] - tsums[pl.ds(o, 1), :]
    forward(3)
    acc3 = acc3 + term(3, p2)
    wait(block_of(3), r_gr.at[3])
    ghsend[lanes(3), :] = (acc3 + term(3, p3)).astype(BF16)
    give_back(3)
    for c in range(4):
        at = slice(c * cols, (c + 1) * cols)
        gw_ref[at, :] = (
            gw_acc[at, :] + jnp.dot(g_all[at, half:], rows[half:, at_part(r)], preferred_element_type=F32)
        ).astype(BF16)
    wait(ghrecv.at[0 : (n - 1) * depth], r_gh)
    gh_ref[...] = lax.dot_general(pack, ghrecv[...], TN, preferred_element_type=F32)
    wait(hidden, s_hx)
    wait(metas.at[0 : n - 1], s_meta)
    wait(sendbuf.at[0 : n - 1], s_row)
    wait(sendbuf.at[0 : n - 1], s_rowx)
    wait(wfull.at[:, 0 : 3 * part], s_w)
    wait(rows.at[:, 0:part], s_fc)
    wait(rows.at[:, 0:part], s_fr)
    wait(statrep.at[0:3], s_sr)
    wait(statown.at[0 : n - 1], s_so)
    for sem in (s_gx, s_gc, s_gr):
        wait(e_all.at[:, 0:cols, :], sem)
    wait(ghsend.at[0 : (n - 1) * depth], s_gh)


def finish(loss_in, gh_in, gw_in, loss_out, gh_out, gw_out, sem):
    moves = [
        pltpu.make_async_copy(a, b, sem.at[i])
        for i, (a, b) in enumerate(((gw_in, gw_out), (gh_in, gh_out), (loss_in, loss_out)))
    ]
    for c in moves:
        c.start()
    for c in moves:
        c.wait()


def fused(hidden, weight, bucket_map, active, label_pick):
    samples, part = hidden.shape
    labels = weight.shape[1]
    n = bucket_map.shape[0]
    depth = 2 * samples * active.shape[1] // n
    cols = labels // 4
    row_count = n * depth
    vmem = pl.BlockSpec(memory_space=pltpu.VMEM)
    hbm = pl.BlockSpec(memory_space=pltpu.HBM)
    dma = pltpu.SemaphoreType.DMA
    sems = [dma((6,))]
    for received in (None, None, 2, None, n - 1, None, None, None, None, n // 2, None, n // 2, None):
        sems += [dma, dma if received is None else dma((received,))]
    loss, grad_hidden, grad_weight = pl.pallas_call(
        functools.partial(kernel, n, depth),
        out_shape=(
            pltpu.VMEM((1, samples), F32),
            pltpu.VMEM((samples, part), F32),
            pltpu.VMEM((labels, part), BF16),
        ),
        in_specs=[hbm] * 5,
        out_specs=(vmem, vmem, vmem),
        scratch_shapes=[
            pltpu.VMEM((2, samples), jnp.int32),
            pltpu.VMEM((1, samples), jnp.int32),
            pltpu.VMEM((1, n), jnp.int32),
            pltpu.VMEM((8, samples), jnp.int32),
            pltpu.VMEM((samples, part), BF16),
            pltpu.VMEM((samples, part), BF16),
            pltpu.VMEM((labels, part), BF16),
            pltpu.VMEM((n, 8, samples), jnp.int32),
            pltpu.VMEM((cols, 4 * part), BF16),
            pltpu.VMEM((n, depth, part), BF16),
            pltpu.VMEM((n, depth, part), BF16),
            pltpu.VMEM((row_count, 4 * part), BF16),
            pltpu.VMEM((2 * n, samples), F32),
            pltpu.VMEM((4, 2 * n, samples), F32),
            pltpu.VMEM((n, samples), F32),
            pltpu.VMEM((n, n, samples), F32),
            pltpu.VMEM((n, samples), F32),
            pltpu.VMEM((n, samples), F32),
            pltpu.VMEM((8, samples), jnp.int32),
            pltpu.VMEM((8, samples), F32),
            pltpu.VMEM((8, samples), F32),
            pltpu.VMEM((n // 2, labels, 2 * depth), BF16),
            pltpu.VMEM((labels, row_count), BF16),
            pltpu.VMEM((labels, part), F32),
            pltpu.VMEM((row_count, part), BF16),
            pltpu.VMEM((row_count, part), BF16),
        ] + sems,
        compiler_params=pltpu.CompilerParams(
            collective_id=0, has_side_effects=True, vmem_limit_bytes=60 * 1024 * 1024
        ),
    )(active.T, label_pick[None], bucket_map[None], hidden, weight[0])
    loss, grad_hidden, grad_weight = pl.pallas_call(
        finish,
        out_shape=(
            jax.ShapeDtypeStruct((1, samples), F32),
            jax.ShapeDtypeStruct((samples, part), F32),
            jax.ShapeDtypeStruct((labels, part), BF16),
        ),
        in_specs=[vmem] * 3,
        out_specs=(hbm, hbm, hbm),
        scratch_shapes=[dma((3,))],
        compiler_params=pltpu.CompilerParams(vmem_limit_bytes=1024 * 1024),
    )(loss, grad_hidden, grad_weight)
    return loss[0], grad_hidden, grad_weight[None]


def body(hidden, weight, bucket_map, active, label_pick):
    samp_count = hidden.shape[0]
    bucket_dev, label_count, feature_part = weight.shape
    picks = active.shape[1]
    bucket_total = bucket_map.shape[0]
    owner_count = lax.axis_size("own")
    slot_depth = max(2, 2 * samp_count * picks // bucket_total)
    pair_count = samp_count * picks
    slots_total = bucket_total * slot_depth
    row_count = owner_count * slot_depth
    pair_bucket = active.reshape(pair_count)
    bucket_iota = lax.broadcasted_iota(jnp.int32, (pair_count, bucket_total), 1)
    slot_index = jnp.sum(
        jnp.where(pair_bucket[:, None] == bucket_iota, bucket_map[None, :], 0), axis=1
    )
    slot_hits = (slot_index[:, None] == bucket_iota).astype(jnp.int32)
    before = lax.broadcasted_iota(jnp.int32, (pair_count, pair_count), 0)
    after = lax.broadcasted_iota(jnp.int32, (pair_count, pair_count), 1)
    earlier = jnp.dot(
        (after < before).astype(BF16), slot_hits.astype(BF16), preferred_element_type=F32
    ).astype(jnp.int32)
    rank_within = jnp.sum(earlier * slot_hits, axis=1)
    position = slot_index * slot_depth + rank_within
    pair_index = jnp.arange(pair_count, dtype=jnp.int32)
    pick_value = jnp.repeat(label_pick, picks)
    target_pair = jnp.where(
        pick_value // label_count == pair_index % picks, pick_value % label_count, -1
    )
    width_sent = hidden.shape[1]
    pair_rows = jnp.repeat(hidden, picks, axis=0)
    send_rows = jnp.zeros((slots_total, width_sent), jnp.bfloat16).at[position].set(pair_rows)
    send_target = jnp.full((slots_total,), -1, jnp.int32).at[position].set(target_pair)
    got_rows, got_target = (
        lax.all_to_all(
            send_rows.reshape(owner_count, bucket_dev * slot_depth, width_sent),
            "own",
            split_axis=0,
            concat_axis=0,
            tiled=True,
        ),
        lax.all_to_all(
            send_target.reshape(owner_count, bucket_dev * slot_depth),
            "own",
            split_axis=0,
            concat_axis=0,
            tiled=True,
        ),
    )
    received = got_rows.reshape(owner_count, bucket_dev, slot_depth, width_sent).transpose(
        1, 0, 2, 3
    )
    received = received.reshape(bucket_dev, row_count, width_sent)
    target_col = (
        got_target.reshape(owner_count, bucket_dev, slot_depth)
        .transpose(1, 0, 2)
        .reshape(bucket_dev, row_count)
    )
    partial_value = jnp.einsum("brd,bcd->brc", received, weight, preferred_element_type=jnp.float32)
    logits = lax.psum(partial_value, "rep")
    columns = lax.broadcasted_iota(jnp.int32, (1, 1, label_count), 2)
    row_max = jnp.max(logits, axis=2)
    row_sum = jnp.sum(jnp.exp(logits - row_max[..., None]), axis=2)
    row_target = jnp.sum(jnp.where(columns == target_col[..., None], logits, 0.0), axis=2)

    def to_sources(values):
        return (
            values.reshape(bucket_dev, owner_count, slot_depth)
            .transpose(1, 0, 2)
            .reshape(owner_count, bucket_dev * slot_depth)
        )

    back_max, back_sum, back_target = (
        lax.all_to_all(to_sources(row_max), "own", split_axis=0, concat_axis=0, tiled=True),
        lax.all_to_all(to_sources(row_sum), "own", split_axis=0, concat_axis=0, tiled=True),
        lax.all_to_all(to_sources(row_target), "own", split_axis=0, concat_axis=0, tiled=True),
    )
    pair_max = back_max.reshape(slots_total)[position].reshape(samp_count, picks)
    pair_sum = back_sum.reshape(slots_total)[position].reshape(samp_count, picks)
    pair_target = back_target.reshape(slots_total)[position].reshape(samp_count, picks)
    peak_max = jnp.max(pair_max, axis=1)
    norm_sum = jnp.sum(pair_sum * jnp.exp(pair_max - peak_max[:, None]), axis=1)
    log_norm = peak_max + jnp.log(norm_sum)
    sample_loss = log_norm - jnp.sum(pair_target, axis=1)
    send_norm = jnp.zeros((slots_total,), jnp.float32).at[position].set(jnp.repeat(log_norm, picks))
    got_norm = lax.all_to_all(
        send_norm.reshape(owner_count, bucket_dev * slot_depth),
        "own",
        split_axis=0,
        concat_axis=0,
        tiled=True,
    )
    row_norm = (
        got_norm.reshape(owner_count, bucket_dev, slot_depth)
        .transpose(1, 0, 2)
        .reshape(bucket_dev, row_count)
    )
    onehot = (columns == target_col[..., None]).astype(jnp.float32)
    grad_logits = (jnp.exp(logits - row_norm[..., None]) - onehot).astype(jnp.bfloat16)
    grad_weight = jnp.einsum(
        "brc,brd->bcd", grad_logits, received, preferred_element_type=jnp.float32
    ).astype(jnp.bfloat16)
    row_grads = jnp.einsum("brc,bcd->brd", grad_logits, weight, preferred_element_type=jnp.float32)
    send_grads = row_grads.reshape(bucket_dev, owner_count, slot_depth, feature_part).transpose(
        1, 0, 2, 3
    )
    send_grads = send_grads.reshape(owner_count, bucket_dev * slot_depth, feature_part)
    got_grads = lax.all_to_all(send_grads, "own", split_axis=0, concat_axis=0, tiled=True)
    pair_grads = got_grads.reshape(slots_total, feature_part)[position].reshape(
        samp_count, picks, feature_part
    )
    grad_hidden = jnp.sum(pair_grads, axis=1)
    return (sample_loss, grad_hidden, grad_weight)


def choose(hidden, weight, bucket_map, active, label_pick):
    samples, picks = active.shape
    buckets = bucket_map.shape[0]
    depth = 2 * samples * picks // buckets
    fits = (
        weight.shape[0] == 1
        and lax.axis_size("rep") == 4
        and buckets == 8
        and picks == 2
        and samples == 128
        and 2 * depth == samples
        and weight.shape[1] % 512 == 0
        and hidden.shape[1] % 128 == 0
    )
    run = fused if fits else body
    return run(hidden, weight, bucket_map, active, label_pick)


def solution(mesh):
    in_specs = (P("own", "rep"), P("own", None, "rep"), P(), P("own", None), P("own"))
    out_specs = (P("own"), P("own", "rep"), P("own", None, "rep"))
    return jax.shard_map(choose, mesh=mesh, in_specs=in_specs, out_specs=out_specs, check_vma=False)
```

```python
import functools
import jax
import jax.numpy as jnp
from jax import lax
from jax.experimental import pallas as pl
from jax.experimental.pallas import tpu as pltpu
from jax.sharding import PartitionSpec as P

MESH = pl.DeviceIdType.MESH
F32 = jnp.float32
BF16 = jnp.bfloat16
NT = (((1,), (1,)), ((), ()))
TN = (((0,), (0,)), ((), ()))


def ranks(slot0, slot1, buckets, upper):
    sources, samples = slot0.shape
    bucket = lax.broadcasted_iota(jnp.int32, (buckets, samples), 0)
    hits = [
        jnp.where((slot0[s : s + 1] == bucket) | (slot1[s : s + 1] == bucket), 1.0, 0.0)
        for s in range(sources)
    ]
    hits = jnp.concatenate(hits, axis=0) if sources > 1 else hits[0]
    earlier = jnp.dot(hits.astype(BF16), upper, preferred_element_type=F32)
    return jnp.where(hits > 0.5, earlier, -1.0).astype(jnp.int32)


def lane_pick(values, index):
    return jnp.take_along_axis(values, index, axis=1)


def kernel(
    n, depth, act_hbm, pick_hbm, map_hbm, hidden_hbm, weight_hbm,
    loss_ref, gh_ref, gw_ref,
    act, pick_own, table_in, meta, hidden, hidden_x, weight, metas, wfull, sendbuf, sendbuf_x, rows, stats, statrep, comb, statown,
    norms, tsums, row_target, row_valid, row_norm, e_all, g_all, hot, u_acc, t_acc, s_mat, ghsend, ghrecv,
    s_loc, s_hx, r_hx, s_meta, r_meta, s_w, r_w, s_row, r_row, s_rowx, r_rowx, s_fr, r_fr,
    s_sr, r_sr, s_so, r_so, s_gx, r_gx, s_gc, r_gc, s_gr, r_gr, s_gh, r_gh,
):
    labels, part = weight_hbm.shape
    samples = hidden_hbm.shape[0]
    cols = labels // 4
    pairs = n // 2
    o = lax.axis_index("own")
    r = lax.axis_index("rep")
    z = o // 2
    y = o - 2 * z
    p1 = r + 1 - 2 * lax.rem(r, 2)
    p2 = lax.rem(r + 2, 4)
    p3 = lax.rem(p1 + 2, 4)
    row_count = n * depth
    local = [
        pltpu.make_async_copy(act_hbm, act, s_loc.at[0]),
        pltpu.make_async_copy(hidden_hbm, hidden, s_loc.at[1]),
        pltpu.make_async_copy(weight_hbm, weight, s_loc.at[2]),
        pltpu.make_async_copy(
            weight_hbm.at[pl.ds(pl.multiple_of(r * cols, cols), cols)],
            wfull.at[:, pl.ds(pl.multiple_of(r * part, part), part)],
            s_loc.at[3],
        ),
        pltpu.make_async_copy(pick_hbm, pick_own, s_loc.at[4]),
        pltpu.make_async_copy(map_hbm, table_in, s_loc.at[5]),
    ]

    def send(src, dst, ssem, rsem, own, rep):
        copy = pltpu.make_async_remote_copy(
            src_ref=src, dst_ref=dst, send_sem=ssem, recv_sem=rsem,
            device_id={"own": own, "rep": rep}, device_id_type=MESH,
        )
        copy.start()

    def wait(ref, sem):
        pltpu.make_async_copy(ref, ref, sem).wait()

    peers = []
    for turned in (pairs - 1 - z, lax.rem(z + 2, pairs), z + 1 - 2 * lax.rem(z, 2)):
        peers += [2 * turned, 2 * turned + 1]
    peers.append(2 * z + 1 - y)

    def at_rows(s):
        return pl.ds(pl.multiple_of(s * depth, depth), depth)

    def takers(p):
        to = 2 * lax.rem(z - 1 - p + 2 * pairs, pairs)
        return (to, to + 1) if p < pairs - 1 else (to + 1 - y,)

    def pair_at(p):
        return lax.rem(z + 1 + p, pairs)

    def at_part(q):
        return pl.ds(pl.multiple_of(q * part, part), part)

    unit = cols // 4
    pieces = ((0, cols - unit), (cols - unit, unit))

    def at_cols(q, start=0, size=None):
        size = cols if size is None else size
        return pl.ds(pl.multiple_of(q * cols + start, unit), size)

    def lanes(p):
        return slice(p * 2 * depth, (p + 1) * 2 * depth)

    barrier = pltpu.get_barrier_semaphore()
    for to in peers:
        pl.semaphore_signal(barrier, inc=1, device_id={"own": to, "rep": r}, device_id_type=MESH)
    for q in (p1, p2, p3):
        pl.semaphore_signal(barrier, inc=1, device_id={"own": o, "rep": q}, device_id_type=MESH)
    for c in local:
        c.start()
    local[0].wait()
    local[4].wait()
    local[5].wait()
    meta[0:2, :] = act[...]
    meta[2:3, :] = pick_own[...]
    meta[3:8, :] = jnp.zeros((5, samples), jnp.int32)
    meta[3:4, 0:n] = table_in[...]
    local[1].wait()
    below = lax.broadcasted_iota(jnp.int32, (samples, samples), 0)
    right = lax.broadcasted_iota(jnp.int32, (samples, samples), 1)
    upper = jnp.where(below < right, 1.0, 0.0).astype(BF16)

    def slots(ids):
        table = jnp.broadcast_to(meta[3:4, :], (n, samples))
        return lane_pick(table, jnp.broadcast_to(ids, (n, samples)))[: ids.shape[0]]

    mine = meta[...]
    own_rank = ranks(slots(mine[0:1]), slots(mine[1:2]), n, upper)
    place = lax.broadcasted_iota(jnp.int32, (depth, samples), 0)
    pack = jnp.concatenate(
        [jnp.where(own_rank[b : b + 1] == place, 1.0, 0.0).astype(BF16) for b in range(n)], axis=0
    )
    packed = jnp.dot(pack, hidden[...], preferred_element_type=F32).astype(BF16)
    for b in range(n):
        sendbuf[b] = packed[b * depth : (b + 1) * depth]
    pl.semaphore_wait(barrier, n - 1 + 3)
    send(hidden_hbm, hidden_x, s_hx, r_hx, o, p2)
    for to in peers:
        send(meta, metas.at[o], s_meta, r_meta, to, r)
    for p in (3, 0, 1, 2):
        for to in takers(p):
            send(sendbuf.at[to], rows.at[at_rows(2 * p + y), at_part(r)], s_row, r_row.at[p], to, r)
    for j, (start, size) in enumerate(pieces):
        for q in (p2, p3, p1):
            send(weight_hbm.at[at_cols(q, start, size)], wfull.at[start : start + size, at_part(r)], s_w, r_w.at[j], o, q)
    own_rows = at_rows(2 * (pairs - 1) + y)
    rows[own_rows, at_part(r)] = sendbuf[o]
    metas[o] = mine

    wait(hidden_x, r_hx)
    packed_x = jnp.dot(pack, hidden_x[...], preferred_element_type=F32).astype(BF16)
    for b in range(n):
        sendbuf_x[b] = packed_x[b * depth : (b + 1) * depth]
    for p in (3, 0, 1, 2):
        for to in takers(p):
            send(sendbuf_x.at[to], rows.at[at_rows(2 * p + y), at_part(p2)], s_rowx, r_rowx.at[p], to, r)
    rows[own_rows, at_part(p2)] = sendbuf_x[o]

    wait(metas.at[0 : n - 1], r_meta)
    slot0 = slots(metas[:, 0, :])
    slot1 = slots(metas[:, 1, :])
    pick = metas[:, 2, :]
    rank_all = ranks(slot0, slot1, n, upper)
    wanted = jnp.where(pick < labels, slot0, slot1)
    code = jnp.where(wanted == o, jnp.where(pick < labels, pick, pick - labels) + 1, 0)
    code_hi = (code // 64).astype(F32)
    code_lo = (code - (code // 64) * 64).astype(F32)
    lane = lax.broadcasted_iota(jnp.int32, (1, samples), 1)
    sub = lax.broadcasted_iota(jnp.int32, (8, samples), 0)
    bucket_sub = lax.broadcasted_iota(jnp.int32, (n, samples), 0)
    row_index = []
    place2 = lax.broadcasted_iota(jnp.int32, (2 * depth, samples), 0)
    for sp in range(pairs):
        info = jnp.zeros((8, 2 * depth), F32)
        for h in range(2):
            s = 2 * sp + h
            rank_me = jnp.max(
                jnp.where(bucket_sub == o, rank_all[s * n : (s + 1) * n], -1), axis=0, keepdims=True
            )
            member = jnp.where(
                (rank_me >= 0) & (rank_me + h * depth == place2), 1.0, 0.0
            ).astype(BF16)
            facts = jnp.where(
                sub == 0, lane.astype(F32),
                jnp.where(sub == 1, code_hi[s : s + 1], jnp.where(sub == 2, code_lo[s : s + 1], jnp.where(sub == 3, 1.0, 0.0))),
            ).astype(BF16)
            info = info + lax.dot_general(facts, member, NT, preferred_element_type=F32)
        row_index.append(info[0:1].astype(jnp.int32))
        row_valid[sp : sp + 1, :] = info[3:4]
        row_target[sp : sp + 1, :] = (info[1:2] * 64.0 + info[2:3]).astype(jnp.int32) - 1
    targets_at = [row_target[pl.ds(pair_at(p), 1), :] for p in range(pairs)]
    target_row = jnp.concatenate(targets_at, axis=1)

    def hand_over(p, q, sem):
        got = lanes(p) if p < pairs - 1 else at_rows(2 * p + 1 - y)
        wait(rows.at[got, at_part(q)], sem.at[p])
        block = rows.at[lanes(p), at_part(q)]
        send(block, block, s_fr, r_fr.at[p], o, p1)

    hand_over(3, r, r_row)
    hand_over(3, p2, r_rowx)
    local[2].wait()
    local[3].wait()
    for c in range(4):
        at = slice(c * cols, (c + 1) * cols)
        ids = lax.broadcasted_iota(jnp.int32, (cols, row_count), 0) + c * cols
        hot[at, :] = jnp.where(ids == target_row, 1.0, 0.0).astype(BF16)
    for p in range(pairs):
        t_acc[lanes(p), :] = lax.dot_general(hot[:, lanes(p)], weight[...], TN, preferred_element_type=F32)
    for p in range(3):
        hand_over(p, r, r_row)

    def pass_x(p, start, size, turn):
        block = e_all.at[p, at_cols(r, start, size), :]
        send(block, block, s_gx, r_gx.at[turn], o, p2)

    def pass_c(p, start, size):
        block = e_all.at[p, at_cols(r, start, size), :]
        send(block, block, s_gc, r_gc, o, p1)

    def scores(first, last, start, size):
        at = slice(first * 2 * depth, last * 2 * depth)
        width = (last - first) * 2 * depth
        logits = lax.dot_general(wfull[start : start + size, :], rows[at, :], NT, preferred_element_type=F32)
        top = jnp.max(logits, axis=0, keepdims=True)
        raised = jnp.exp(logits - top)
        for p in range(first, last):
            e_all[p, at_cols(r, start, size), :] = raised[:, (p - first) * 2 * depth : (p - first + 1) * 2 * depth].astype(BF16)
        if first == 3 and start == 0:
            pass_x(3, start, size, 3)
        if first == 0:
            pass_x(0, *pieces[0], 0)
        label_id = lax.broadcasted_iota(jnp.int32, (size, width), 0) + (r * cols + start)
        target = jnp.sum(jnp.where(label_id == target_row[:, at], logits, 0.0), axis=0, keepdims=True)
        return top, jnp.sum(raised, axis=0, keepdims=True), target

    for j, (start, size) in enumerate(pieces):
        wait(wfull.at[start : start + size, 0 : 3 * part], r_w.at[j])
        if j == 0:
            wait(rows.at[lanes(3), 0 : 2 * part], r_fr.at[3])
            top_a, sum_a, target_a = scores(3, 4, start, size)
            pass_c(3, start, size)
            for p in range(3):
                hand_over(p, p2, r_rowx)
        else:
            wait(rows.at[lanes(0), 0 : 2 * part], r_fr.at[0])
            first = scores(0, 1, 0, cols)
            wait(rows.at[lanes(1), 0 : 2 * part], r_fr.at[1])
            wait(rows.at[lanes(2), 0 : 2 * part], r_fr.at[2])
            second = scores(1, 3, 0, cols)
            top_b, sum_b, target_b = scores(3, 4, start, size)
    top_r, sum_r, target_r = (jnp.concatenate(x, axis=1) for x in zip(first, second))
    peak = jnp.maximum(top_a, top_b)
    lse_d = peak + jnp.log(sum_a * jnp.exp(top_a - peak) + sum_b * jnp.exp(top_b - peak))
    lse = jnp.concatenate([top_r + jnp.log(sum_r), lse_d], axis=1)
    target_sum = jnp.concatenate([target_r, target_a + target_b], axis=1)
    tops = [jnp.concatenate([top_r, top_a], axis=1), jnp.concatenate([top_r, top_b], axis=1)]
    for p in range(pairs):
        stats[p : p + 1, :] = lse[:, lanes(p)]
        stats[pairs + p : pairs + p + 1, :] = target_sum[:, lanes(p)]
        stats[n + p : n + p + 1, :] = tops[0][:, lanes(p)]
        stats[n + pairs + p : n + pairs + p + 1, :] = tops[1][:, lanes(p)]
    for q in (p2, p3, p1):
        send(stats, statrep.at[r], s_sr, r_sr, o, q)
    pass_x(0, *pieces[1], 0)
    pass_x(1, 0, cols, 1)
    pass_x(2, 0, cols, 2)
    pass_x(3, *pieces[1], 4)
    for p in range(3):
        pass_c(p, 0, cols)
    pass_c(3, *pieces[1])
    statrep[r] = stats[...]
    wait(statrep.at[0:3], r_sr)
    parts = [statrep[q, 0:n, :] for q in range(4)]
    high = jnp.maximum(jnp.maximum(parts[0], parts[1]), jnp.maximum(parts[2], parts[3]))
    total = high + jnp.log(sum(jnp.exp(x - high) for x in parts))
    summed = sum(parts)
    for p in range(pairs):
        comb[pl.ds(pair_at(p), 1), :] = total[p : p + 1]
        comb[pl.ds(pairs + pair_at(p), 1), :] = summed[pairs + p : pairs + p + 1]
    for to in peers:
        send(comb, statown.at[o], s_so, r_so, to, r)
    statown[o] = comb[...]

    def forward(p, start, size, turn):
        block = e_all.at[p, at_cols(p2, start, size), :]
        wait(block, r_gx.at[turn])
        send(block, block, s_gr, r_gr.at[turn], o, p1)

    def handed(p, start, size, turn):
        wait(e_all.at[p, at_cols(p3, start, size), :], r_gr.at[turn])

    highs = []
    for p in range(pairs):
        seen = [statrep[q, n + j * pairs + p : n + j * pairs + p + 1, :] for q in range(4) for j in range(2)]
        highs.append(functools.reduce(jnp.maximum, seen))

    def term(p, q, spans):
        for start, size in spans:
            at = at_cols(q, start, size)
            base = n + (pairs if start else 0) + p
            top = statrep[pl.ds(q, 1), base : base + 1, :].reshape(1, samples)
            g_all[at, lanes(p)] = (e_all[p, at, :].astype(F32) * jnp.exp(top - highs[p])).astype(BF16)
        first, size = spans[0][0], sum(x for _, x in spans)
        at = at_cols(q, first, size)
        return lax.dot_general(g_all[at, lanes(p)], weight[at, :], TN, preferred_element_type=F32)

    whole = ((0, cols),)
    wait(e_all.at[:, at_cols(p1), :], r_gc)
    forward(3, *pieces[0], 3)
    for p in range(pairs):
        spans = whole if p < 3 else pieces
        u_acc[lanes(p), :] = term(p, r, spans) + term(p, p1, spans)
    forward(0, 0, cols, 0)
    u_acc[lanes(0), :] += term(0, p2, whole)
    u_acc[lanes(3), :] += term(3, p2, pieces[:1])
    handed(3, *pieces[0], 3)
    u_acc[lanes(3), :] += term(3, p3, pieces[:1])
    handed(0, 0, cols, 0)
    u_acc[lanes(0), :] += term(0, p3, whole)
    forward(1, 0, cols, 1)
    u_acc[lanes(1), :] += term(1, p2, whole)
    wait(statown.at[0 : n - 1], r_so)
    for sp in range(pairs):
        held = statown[:, sp, :]
        pair = []
        for h in range(2):
            s = 2 * sp + h
            rank = rank_all[s * n : (s + 1) * n]
            index = jnp.where(rank >= 0, rank + h * depth, 0)
            value = jnp.where(rank >= 0, lane_pick(held, index), -3.0e38)
            most = jnp.max(value, axis=0, keepdims=True)
            norm = most + jnp.log(jnp.sum(jnp.exp(value - most), axis=0, keepdims=True))
            norms[s : s + 1, :] = norm
            pair.append(
                lane_pick(jnp.broadcast_to(norm, (8, samples)), jnp.broadcast_to(row_index[sp], (8, samples)))[0:1]
            )
        row_norm[sp : sp + 1, :] = jnp.where(lane < depth, pair[0], pair[1])
    scales = []
    for p in range(pairs):
        norm = row_norm[pl.ds(pair_at(p), 1), :]
        valid = row_valid[pl.ds(pair_at(p), 1), :] > 0.5
        scale = jnp.where(valid, jnp.exp(highs[p] - norm), 0.0)
        scales.append(scale)
        s_mat[lanes(p), :] = jnp.transpose(jnp.broadcast_to(scale, (2 * depth, samples)))

    def scaled(values, p):
        return values * jnp.concatenate([s_mat[lanes(p), :]] * (part // samples), axis=1)

    def give_back(p):
        ghsend[lanes(p), :] = (scaled(u_acc[lanes(p), :], p) - t_acc[lanes(p), :]).astype(BF16)
        if p < pairs - 1:
            for h in range(2):
                at = slice((2 * p + h) * depth, (2 * p + h + 1) * depth)
                send(ghsend.at[at], ghrecv.at[at_rows(o)], s_gh, r_gh, 2 * pair_at(p) + h, r)
        else:
            send(ghsend.at[at_rows(2 * p + 1 - y)], ghrecv.at[at_rows(o)], s_gh, r_gh, 2 * z + 1 - y, r)
            ghrecv[at_rows(o), :] = ghsend[at_rows(2 * p + y), :]

    give_back(0)
    handed(1, 0, cols, 1)
    u_acc[lanes(1), :] += term(1, p3, whole)
    give_back(1)
    forward(2, 0, cols, 2)
    u_acc[lanes(2), :] += term(2, p2, whole)
    handed(2, 0, cols, 2)
    u_acc[lanes(2), :] += term(2, p3, whole)
    give_back(2)
    for sp in range(pairs):
        held = statown[:, pairs + sp, :]
        for h in range(2):
            s = 2 * sp + h
            rank = rank_all[s * n : (s + 1) * n]
            index = jnp.where(rank >= 0, rank + h * depth, 0)
            value = jnp.where(rank >= 0, lane_pick(held, index), 0.0)
            tsums[s : s + 1, :] = jnp.sum(value, axis=0, keepdims=True)
    loss_ref[...] = norms[pl.ds(o, 1), :] - tsums[pl.ds(o, 1), :]
    forward(3, *pieces[1], 4)
    u_acc[lanes(3), :] += term(3, p2, pieces[1:])
    handed(3, *pieces[1], 4)
    u_acc[lanes(3), :] += term(3, p3, pieces[1:])
    give_back(3)
    scale_row = jnp.concatenate(scales, axis=1)
    for c in range(4):
        at = slice(c * cols, (c + 1) * cols)
        grad = g_all[at, :].astype(F32) * scale_row - hot[at, :].astype(F32)
        gw_ref[at, :] = jnp.dot(grad.astype(BF16), rows[:, at_part(r)], preferred_element_type=F32).astype(BF16)
    wait(ghrecv.at[0 : (n - 1) * depth], r_gh)
    gh_ref[...] = lax.dot_general(pack, ghrecv[...], TN, preferred_element_type=F32)
    wait(hidden, s_hx)
    wait(metas.at[0 : n - 1], s_meta)
    wait(sendbuf.at[0 : n - 1], s_row)
    wait(sendbuf.at[0 : n - 1], s_rowx)
    wait(wfull.at[:, 0 : 3 * part], s_w)
    wait(rows.at[:, 0 : 2 * part], s_fr)
    wait(statrep.at[0:3], s_sr)
    wait(statown.at[0 : n - 1], s_so)
    for sem in (s_gx, s_gc, s_gr):
        wait(e_all.at[:, 0:cols, :], sem)
    wait(ghsend.at[0 : (n - 1) * depth], s_gh)


def finish(loss_in, gh_in, gw_in, loss_out, gh_out, gw_out, sem):
    moves = [
        pltpu.make_async_copy(a, b, sem.at[i])
        for i, (a, b) in enumerate(((gw_in, gw_out), (gh_in, gh_out), (loss_in, loss_out)))
    ]
    for c in moves:
        c.start()
    for c in moves:
        c.wait()


def fused(hidden, weight, bucket_map, active, label_pick):
    samples, part = hidden.shape
    labels = weight.shape[1]
    n = bucket_map.shape[0]
    depth = 2 * samples * active.shape[1] // n
    cols = labels // 4
    row_count = n * depth
    vmem = pl.BlockSpec(memory_space=pltpu.VMEM)
    hbm = pl.BlockSpec(memory_space=pltpu.HBM)
    dma = pltpu.SemaphoreType.DMA
    sems = [dma((6,))]
    for received in (None, None, 2, n // 2, n // 2, n // 2, None, None, n // 2 + 1, None, n // 2 + 1, None):
        sems += [dma, dma if received is None else dma((received,))]
    loss, grad_hidden, grad_weight = pl.pallas_call(
        functools.partial(kernel, n, depth),
        out_shape=(
            pltpu.VMEM((1, samples), F32),
            pltpu.VMEM((samples, part), F32),
            pltpu.VMEM((labels, part), BF16),
        ),
        in_specs=[hbm] * 5,
        out_specs=(vmem, vmem, vmem),
        scratch_shapes=[
            pltpu.VMEM((2, samples), jnp.int32),
            pltpu.VMEM((1, samples), jnp.int32),
            pltpu.VMEM((1, n), jnp.int32),
            pltpu.VMEM((8, samples), jnp.int32),
            pltpu.VMEM((samples, part), BF16),
            pltpu.VMEM((samples, part), BF16),
            pltpu.VMEM((labels, part), BF16),
            pltpu.VMEM((n, 8, samples), jnp.int32),
            pltpu.VMEM((cols, 4 * part), BF16),
            pltpu.VMEM((n, depth, part), BF16),
            pltpu.VMEM((n, depth, part), BF16),
            pltpu.VMEM((row_count, 4 * part), BF16),
            pltpu.VMEM((2 * n, samples), F32),
            pltpu.VMEM((4, 2 * n, samples), F32),
            pltpu.VMEM((n, samples), F32),
            pltpu.VMEM((n, n, samples), F32),
            pltpu.VMEM((n, samples), F32),
            pltpu.VMEM((n, samples), F32),
            pltpu.VMEM((8, samples), jnp.int32),
            pltpu.VMEM((8, samples), F32),
            pltpu.VMEM((8, samples), F32),
            pltpu.VMEM((n // 2, labels, 2 * depth), BF16),
            pltpu.VMEM((labels, row_count), BF16),
            pltpu.VMEM((labels, row_count), BF16),
            pltpu.VMEM((row_count, part), F32),
            pltpu.VMEM((row_count, part), F32),
            pltpu.VMEM((row_count, samples), F32),
            pltpu.VMEM((row_count, part), BF16),
            pltpu.VMEM((row_count, part), BF16),
        ] + sems,
        compiler_params=pltpu.CompilerParams(
            collective_id=0, has_side_effects=True, vmem_limit_bytes=60 * 1024 * 1024
        ),
    )(active.T, label_pick[None], bucket_map[None], hidden, weight[0])
    loss, grad_hidden, grad_weight = pl.pallas_call(
        finish,
        out_shape=(
            jax.ShapeDtypeStruct((1, samples), F32),
            jax.ShapeDtypeStruct((samples, part), F32),
            jax.ShapeDtypeStruct((labels, part), BF16),
        ),
        in_specs=[vmem] * 3,
        out_specs=(hbm, hbm, hbm),
        scratch_shapes=[dma((3,))],
        compiler_params=pltpu.CompilerParams(vmem_limit_bytes=1024 * 1024),
    )(loss, grad_hidden, grad_weight)
    return loss[0], grad_hidden, grad_weight[None]


def body(hidden, weight, bucket_map, active, label_pick):
    samp_count = hidden.shape[0]
    bucket_dev, label_count, feature_part = weight.shape
    picks = active.shape[1]
    bucket_total = bucket_map.shape[0]
    owner_count = lax.axis_size("own")
    slot_depth = max(2, 2 * samp_count * picks // bucket_total)
    pair_count = samp_count * picks
    slots_total = bucket_total * slot_depth
    row_count = owner_count * slot_depth
    pair_bucket = active.reshape(pair_count)
    bucket_iota = lax.broadcasted_iota(jnp.int32, (pair_count, bucket_total), 1)
    slot_index = jnp.sum(
        jnp.where(pair_bucket[:, None] == bucket_iota, bucket_map[None, :], 0), axis=1
    )
    slot_hits = (slot_index[:, None] == bucket_iota).astype(jnp.int32)
    before = lax.broadcasted_iota(jnp.int32, (pair_count, pair_count), 0)
    after = lax.broadcasted_iota(jnp.int32, (pair_count, pair_count), 1)
    earlier = jnp.dot(
        (after < before).astype(BF16), slot_hits.astype(BF16), preferred_element_type=F32
    ).astype(jnp.int32)
    rank_within = jnp.sum(earlier * slot_hits, axis=1)
    position = slot_index * slot_depth + rank_within
    pair_index = jnp.arange(pair_count, dtype=jnp.int32)
    pick_value = jnp.repeat(label_pick, picks)
    target_pair = jnp.where(
        pick_value // label_count == pair_index % picks, pick_value % label_count, -1
    )
    width_sent = hidden.shape[1]
    pair_rows = jnp.repeat(hidden, picks, axis=0)
    send_rows = jnp.zeros((slots_total, width_sent), jnp.bfloat16).at[position].set(pair_rows)
    send_target = jnp.full((slots_total,), -1, jnp.int32).at[position].set(target_pair)
    got_rows, got_target = (
        lax.all_to_all(
            send_rows.reshape(owner_count, bucket_dev * slot_depth, width_sent),
            "own",
            split_axis=0,
            concat_axis=0,
            tiled=True,
        ),
        lax.all_to_all(
            send_target.reshape(owner_count, bucket_dev * slot_depth),
            "own",
            split_axis=0,
            concat_axis=0,
            tiled=True,
        ),
    )
    received = got_rows.reshape(owner_count, bucket_dev, slot_depth, width_sent).transpose(
        1, 0, 2, 3
    )
    received = received.reshape(bucket_dev, row_count, width_sent)
    target_col = (
        got_target.reshape(owner_count, bucket_dev, slot_depth)
        .transpose(1, 0, 2)
        .reshape(bucket_dev, row_count)
    )
    partial_value = jnp.einsum("brd,bcd->brc", received, weight, preferred_element_type=jnp.float32)
    logits = lax.psum(partial_value, "rep")
    columns = lax.broadcasted_iota(jnp.int32, (1, 1, label_count), 2)
    row_max = jnp.max(logits, axis=2)
    row_sum = jnp.sum(jnp.exp(logits - row_max[..., None]), axis=2)
    row_target = jnp.sum(jnp.where(columns == target_col[..., None], logits, 0.0), axis=2)

    def to_sources(values):
        return (
            values.reshape(bucket_dev, owner_count, slot_depth)
            .transpose(1, 0, 2)
            .reshape(owner_count, bucket_dev * slot_depth)
        )

    back_max, back_sum, back_target = (
        lax.all_to_all(to_sources(row_max), "own", split_axis=0, concat_axis=0, tiled=True),
        lax.all_to_all(to_sources(row_sum), "own", split_axis=0, concat_axis=0, tiled=True),
        lax.all_to_all(to_sources(row_target), "own", split_axis=0, concat_axis=0, tiled=True),
    )
    pair_max = back_max.reshape(slots_total)[position].reshape(samp_count, picks)
    pair_sum = back_sum.reshape(slots_total)[position].reshape(samp_count, picks)
    pair_target = back_target.reshape(slots_total)[position].reshape(samp_count, picks)
    peak_max = jnp.max(pair_max, axis=1)
    norm_sum = jnp.sum(pair_sum * jnp.exp(pair_max - peak_max[:, None]), axis=1)
    log_norm = peak_max + jnp.log(norm_sum)
    sample_loss = log_norm - jnp.sum(pair_target, axis=1)
    send_norm = jnp.zeros((slots_total,), jnp.float32).at[position].set(jnp.repeat(log_norm, picks))
    got_norm = lax.all_to_all(
        send_norm.reshape(owner_count, bucket_dev * slot_depth),
        "own",
        split_axis=0,
        concat_axis=0,
        tiled=True,
    )
    row_norm = (
        got_norm.reshape(owner_count, bucket_dev, slot_depth)
        .transpose(1, 0, 2)
        .reshape(bucket_dev, row_count)
    )
    onehot = (columns == target_col[..., None]).astype(jnp.float32)
    grad_logits = (jnp.exp(logits - row_norm[..., None]) - onehot).astype(jnp.bfloat16)
    grad_weight = jnp.einsum(
        "brc,brd->bcd", grad_logits, received, preferred_element_type=jnp.float32
    ).astype(jnp.bfloat16)
    row_grads = jnp.einsum("brc,bcd->brd", grad_logits, weight, preferred_element_type=jnp.float32)
    send_grads = row_grads.reshape(bucket_dev, owner_count, slot_depth, feature_part).transpose(
        1, 0, 2, 3
    )
    send_grads = send_grads.reshape(owner_count, bucket_dev * slot_depth, feature_part)
    got_grads = lax.all_to_all(send_grads, "own", split_axis=0, concat_axis=0, tiled=True)
    pair_grads = got_grads.reshape(slots_total, feature_part)[position].reshape(
        samp_count, picks, feature_part
    )
    grad_hidden = jnp.sum(pair_grads, axis=1)
    return (sample_loss, grad_hidden, grad_weight)


def choose(hidden, weight, bucket_map, active, label_pick):
    samples, picks = active.shape
    buckets = bucket_map.shape[0]
    depth = 2 * samples * picks // buckets
    fits = (
        weight.shape[0] == 1
        and lax.axis_size("rep") == 4
        and buckets == 8
        and picks == 2
        and samples == 128
        and 2 * depth == samples
        and weight.shape[1] % 512 == 0
        and hidden.shape[1] % 128 == 0
    )
    run = fused if fits else body
    return run(hidden, weight, bucket_map, active, label_pick)


def solution(mesh):
    in_specs = (P("own", "rep"), P("own", None, "rep"), P(), P("own", None), P("own"))
    out_specs = (P("own"), P("own", "rep"), P("own", None, "rep"))
    return jax.shard_map(choose, mesh=mesh, in_specs=in_specs, out_specs=out_specs, check_vma=False)
```

```python
import functools
import jax
import jax.numpy as jnp
from jax import lax
from jax.experimental import pallas as pl
from jax.experimental.pallas import tpu as pltpu
from jax.sharding import PartitionSpec as P

MESH = pl.DeviceIdType.MESH
F32 = jnp.float32
BF16 = jnp.bfloat16
NT = (((1,), (1,)), ((), ()))
TN = (((0,), (0,)), ((), ()))


def ranks(slot0, slot1, buckets, upper):
    sources, samples = slot0.shape
    bucket = lax.broadcasted_iota(jnp.int32, (buckets, samples), 0)
    hits = [
        jnp.where((slot0[s : s + 1] == bucket) | (slot1[s : s + 1] == bucket), 1.0, 0.0)
        for s in range(sources)
    ]
    hits = jnp.concatenate(hits, axis=0) if sources > 1 else hits[0]
    earlier = jnp.dot(hits.astype(BF16), upper, preferred_element_type=F32)
    return jnp.where(hits > 0.5, earlier, -1.0).astype(jnp.int32)


def lane_pick(values, index):
    return jnp.take_along_axis(values, index, axis=1)


def kernel(
    n, depth, act_hbm, pick_hbm, map_hbm, hidden_hbm, weight_hbm,
    loss_ref, gh_ref, gw_ref,
    act, pick_own, table_in, meta, hidden, hidden_x, weight, metas, wfull, sendbuf, sendbuf_x, rows, stats, statrep, comb, statown,
    norms, tsums, row_target, row_valid, row_norm, e_all, g_all, hot, u_acc, t_acc, s_mat, ghsend, ghrecv,
    go, s_loc, s_hx, r_hx, s_meta, r_meta, s_w, r_w, s_row, r_row, s_rowx, r_rowx, s_fr, r_fr,
    s_sr, r_sr, s_so, r_so, s_gx, r_gx, s_gc, r_gc, s_gr, r_gr, s_gh, r_gh,
):
    labels, part = weight_hbm.shape
    samples = hidden_hbm.shape[0]
    cols = labels // 4
    pairs = n // 2
    o = lax.axis_index("own")
    r = lax.axis_index("rep")
    z = o // 2
    y = o - 2 * z
    p1 = r + 1 - 2 * lax.rem(r, 2)
    p2 = lax.rem(r + 2, 4)
    p3 = lax.rem(p1 + 2, 4)
    row_count = n * depth
    local = [
        pltpu.make_async_copy(act_hbm, act, s_loc.at[0]),
        pltpu.make_async_copy(hidden_hbm, hidden, s_loc.at[1]),
        pltpu.make_async_copy(weight_hbm, weight, s_loc.at[2]),
        pltpu.make_async_copy(
            weight_hbm.at[pl.ds(pl.multiple_of(r * cols, cols), cols)],
            wfull.at[:, pl.ds(pl.multiple_of(r * part, part), part)],
            s_loc.at[3],
        ),
        pltpu.make_async_copy(pick_hbm, pick_own, s_loc.at[4]),
        pltpu.make_async_copy(map_hbm, table_in, s_loc.at[5]),
    ]

    def send(src, dst, ssem, rsem, own, rep):
        copy = pltpu.make_async_remote_copy(
            src_ref=src, dst_ref=dst, send_sem=ssem, recv_sem=rsem,
            device_id={"own": own, "rep": rep}, device_id_type=MESH,
        )
        copy.start()

    def wait(ref, sem):
        pltpu.make_async_copy(ref, ref, sem).wait()

    peers = []
    for turned in (pairs - 1 - z, lax.rem(z + 2, pairs), z + 1 - 2 * lax.rem(z, 2)):
        peers += [2 * turned, 2 * turned + 1]
    peers.append(2 * z + 1 - y)

    def at_rows(s):
        return pl.ds(pl.multiple_of(s * depth, depth), depth)

    def turn_of(to):
        return lax.rem(z - to // 2 + pairs + pairs - 1, pairs)

    def pair_at(p):
        return lax.rem(z + 1 + p, pairs)

    def at_part(q):
        return pl.ds(pl.multiple_of(q * part, part), part)

    unit = cols // 4
    pieces = ((0, cols - unit), (cols - unit, unit))

    def at_cols(q, start=0, size=None):
        size = cols if size is None else size
        return pl.ds(pl.multiple_of(q * cols + start, unit), size)

    def lanes(p):
        return slice(p * 2 * depth, (p + 1) * 2 * depth)

    barrier = pltpu.get_barrier_semaphore()
    odd = lax.rem(r, 2)
    even = r - odd

    def greet(own, rep):
        pl.semaphore_signal(barrier, inc=1, device_id={"own": own, "rep": rep}, device_id_type=MESH)

    @pl.when(odd == 0)
    def _():
        greet(o, p2)
        greet(o, p1)

    @pl.when(odd == 1)
    def _():
        greet(o, p1)
        greet(o, p3)

    for to in peers:
        greet(to, even + 1)
    for c in local:
        c.start()

    @pl.when(odd == 0)
    def _():
        pl.semaphore_wait(barrier, 3)
        pl.semaphore_signal(go, inc=1, device_id={"own": o, "rep": p1}, device_id_type=MESH)

    @pl.when(odd == 1)
    def _():
        pl.semaphore_wait(go, 1)

    send(hidden_hbm, hidden_x, s_hx, r_hx, o, p2)
    for j, (start, size) in enumerate(pieces):
        for q in (p2, p3, p1):
            send(weight_hbm.at[at_cols(q, start, size)], wfull.at[start : start + size, at_part(r)], s_w, r_w.at[j], o, q)
    local[0].wait()
    local[4].wait()
    local[5].wait()
    meta[0:2, :] = act[...]
    meta[2:3, :] = pick_own[...]
    meta[3:8, :] = jnp.zeros((5, samples), jnp.int32)
    meta[3:4, 0:n] = table_in[...]
    local[1].wait()
    below = lax.broadcasted_iota(jnp.int32, (samples, samples), 0)
    right = lax.broadcasted_iota(jnp.int32, (samples, samples), 1)
    upper = jnp.where(below < right, 1.0, 0.0).astype(BF16)

    def slots(ids):
        table = jnp.broadcast_to(meta[3:4, :], (n, samples))
        return lane_pick(table, jnp.broadcast_to(ids, (n, samples)))[: ids.shape[0]]

    mine = meta[...]
    own_rank = ranks(slots(mine[0:1]), slots(mine[1:2]), n, upper)
    place = lax.broadcasted_iota(jnp.int32, (depth, samples), 0)
    pack = jnp.concatenate(
        [jnp.where(own_rank[b : b + 1] == place, 1.0, 0.0).astype(BF16) for b in range(n)], axis=0
    )
    packed = jnp.dot(pack, hidden[...], preferred_element_type=F32).astype(BF16)
    for b in range(n):
        sendbuf[b] = packed[b * depth : (b + 1) * depth]

    @pl.when(odd == 1)
    def _():
        pl.semaphore_wait(barrier, 2 * (n - 1) + 1)
        pl.semaphore_signal(go, inc=1, device_id={"own": o, "rep": p1}, device_id_type=MESH)

    @pl.when(odd == 0)
    def _():
        pl.semaphore_wait(go, 1)

    for to in peers:
        send(meta, metas.at[o], s_meta, r_meta, to, r)
    row_order = [peers[-1]] + peers[:-1]
    for to in row_order:
        p = turn_of(to)
        send(sendbuf.at[to], rows.at[at_rows(2 * p + y), at_part(r)], s_row, r_row.at[p], to, r)
    own_rows = at_rows(2 * (pairs - 1) + y)
    rows[own_rows, at_part(r)] = sendbuf[o]
    metas[o] = mine

    wait(hidden_x, r_hx)
    packed_x = jnp.dot(pack, hidden_x[...], preferred_element_type=F32).astype(BF16)
    for b in range(n):
        sendbuf_x[b] = packed_x[b * depth : (b + 1) * depth]
    for to in row_order:
        p = turn_of(to)
        send(sendbuf_x.at[to], rows.at[at_rows(2 * p + y), at_part(p2)], s_rowx, r_rowx.at[p], to, r)
    rows[own_rows, at_part(p2)] = sendbuf_x[o]

    wait(metas.at[0 : n - 1], r_meta)
    slot0 = slots(metas[:, 0, :])
    slot1 = slots(metas[:, 1, :])
    pick = metas[:, 2, :]
    rank_all = ranks(slot0, slot1, n, upper)
    wanted = jnp.where(pick < labels, slot0, slot1)
    code = jnp.where(wanted == o, jnp.where(pick < labels, pick, pick - labels) + 1, 0)
    code_hi = (code // 64).astype(F32)
    code_lo = (code - (code // 64) * 64).astype(F32)
    lane = lax.broadcasted_iota(jnp.int32, (1, samples), 1)
    sub = lax.broadcasted_iota(jnp.int32, (8, samples), 0)
    bucket_sub = lax.broadcasted_iota(jnp.int32, (n, samples), 0)
    row_index = []
    place2 = lax.broadcasted_iota(jnp.int32, (2 * depth, samples), 0)
    for sp in range(pairs):
        info = jnp.zeros((8, 2 * depth), F32)
        for h in range(2):
            s = 2 * sp + h
            rank_me = jnp.max(
                jnp.where(bucket_sub == o, rank_all[s * n : (s + 1) * n], -1), axis=0, keepdims=True
            )
            member = jnp.where(
                (rank_me >= 0) & (rank_me + h * depth == place2), 1.0, 0.0
            ).astype(BF16)
            facts = jnp.where(
                sub == 0, lane.astype(F32),
                jnp.where(sub == 1, code_hi[s : s + 1], jnp.where(sub == 2, code_lo[s : s + 1], jnp.where(sub == 3, 1.0, 0.0))),
            ).astype(BF16)
            info = info + lax.dot_general(facts, member, NT, preferred_element_type=F32)
        row_index.append(info[0:1].astype(jnp.int32))
        row_valid[sp : sp + 1, :] = info[3:4]
        row_target[sp : sp + 1, :] = (info[1:2] * 64.0 + info[2:3]).astype(jnp.int32) - 1
    targets_at = [row_target[pl.ds(pair_at(p), 1), :] for p in range(pairs)]
    target_row = jnp.concatenate(targets_at, axis=1)

    def hand_over(p, q, sem):
        got = lanes(p) if p < pairs - 1 else at_rows(2 * p + 1 - y)
        wait(rows.at[got, at_part(q)], sem.at[p])
        block = rows.at[lanes(p), at_part(q)]
        send(block, block, s_fr, r_fr.at[p], o, p1)

    hand_over(3, r, r_row)
    hand_over(3, p2, r_rowx)
    local[2].wait()
    local[3].wait()
    for c in range(4):
        at = slice(c * cols, (c + 1) * cols)
        ids = lax.broadcasted_iota(jnp.int32, (cols, row_count), 0) + c * cols
        hot[at, :] = jnp.where(ids == target_row, 1.0, 0.0).astype(BF16)
    for p in range(pairs):
        t_acc[lanes(p), :] = lax.dot_general(hot[:, lanes(p)], weight[...], TN, preferred_element_type=F32)
    for p in range(3):
        hand_over(p, r, r_row)

    def pass_x(p, start, size, turn):
        block = e_all.at[p, at_cols(r, start, size), :]
        send(block, block, s_gx, r_gx.at[turn], o, p2)

    def pass_c(p, start, size):
        block = e_all.at[p, at_cols(r, start, size), :]
        send(block, block, s_gc, r_gc, o, p1)

    def scores(first, last, start, size):
        at = slice(first * 2 * depth, last * 2 * depth)
        width = (last - first) * 2 * depth
        logits = lax.dot_general(wfull[start : start + size, :], rows[at, :], NT, preferred_element_type=F32)
        top = jnp.max(logits, axis=0, keepdims=True)
        raised = jnp.exp(logits - top)
        for p in range(first, last):
            e_all[p, at_cols(r, start, size), :] = raised[:, (p - first) * 2 * depth : (p - first + 1) * 2 * depth].astype(BF16)
        if first == 3 and start == 0:
            pass_x(3, start, size, 3)
        if first == 0:
            pass_x(0, *pieces[0], 0)
        label_id = lax.broadcasted_iota(jnp.int32, (size, width), 0) + (r * cols + start)
        target = jnp.sum(jnp.where(label_id == target_row[:, at], logits, 0.0), axis=0, keepdims=True)
        return top, jnp.sum(raised, axis=0, keepdims=True), target

    for j, (start, size) in enumerate(pieces):
        wait(wfull.at[start : start + size, 0 : 3 * part], r_w.at[j])
        if j == 0:
            wait(rows.at[lanes(3), 0 : 2 * part], r_fr.at[3])
            top_a, sum_a, target_a = scores(3, 4, start, size)
            pass_c(3, start, size)
            for p in range(3):
                hand_over(p, p2, r_rowx)
        else:
            wait(rows.at[lanes(0), 0 : 2 * part], r_fr.at[0])
            first = scores(0, 1, 0, cols)
            wait(rows.at[lanes(1), 0 : 2 * part], r_fr.at[1])
            wait(rows.at[lanes(2), 0 : 2 * part], r_fr.at[2])
            second = scores(1, 3, 0, cols)
            top_b, sum_b, target_b = scores(3, 4, start, size)
    top_r, sum_r, target_r = (jnp.concatenate(x, axis=1) for x in zip(first, second))
    peak = jnp.maximum(top_a, top_b)
    lse_d = peak + jnp.log(sum_a * jnp.exp(top_a - peak) + sum_b * jnp.exp(top_b - peak))
    lse = jnp.concatenate([top_r + jnp.log(sum_r), lse_d], axis=1)
    target_sum = jnp.concatenate([target_r, target_a + target_b], axis=1)
    tops = [jnp.concatenate([top_r, top_a], axis=1), jnp.concatenate([top_r, top_b], axis=1)]
    for p in range(pairs):
        stats[p : p + 1, :] = lse[:, lanes(p)]
        stats[pairs + p : pairs + p + 1, :] = target_sum[:, lanes(p)]
        stats[n + p : n + p + 1, :] = tops[0][:, lanes(p)]
        stats[n + pairs + p : n + pairs + p + 1, :] = tops[1][:, lanes(p)]
    for q in (p2, p3, p1):
        send(stats, statrep.at[r], s_sr, r_sr, o, q)
    pass_x(0, *pieces[1], 0)
    pass_x(1, 0, cols, 1)
    pass_x(2, 0, cols, 2)
    pass_x(3, *pieces[1], 4)
    for p in range(3):
        pass_c(p, 0, cols)
    pass_c(3, *pieces[1])
    statrep[r] = stats[...]
    wait(statrep.at[0:3], r_sr)
    parts = [statrep[q, 0:n, :] for q in range(4)]
    high = jnp.maximum(jnp.maximum(parts[0], parts[1]), jnp.maximum(parts[2], parts[3]))
    total = high + jnp.log(sum(jnp.exp(x - high) for x in parts))
    summed = sum(parts)
    for p in range(pairs):
        comb[pl.ds(pair_at(p), 1), :] = total[p : p + 1]
        comb[pl.ds(pairs + pair_at(p), 1), :] = summed[pairs + p : pairs + p + 1]
    for to in peers:
        send(comb, statown.at[o], s_so, r_so, to, r)
    statown[o] = comb[...]

    def forward(p, start, size, turn):
        block = e_all.at[p, at_cols(p2, start, size), :]
        wait(block, r_gx.at[turn])
        send(block, block, s_gr, r_gr.at[turn], o, p1)

    def handed(p, start, size, turn):
        wait(e_all.at[p, at_cols(p3, start, size), :], r_gr.at[turn])

    highs = []
    for p in range(pairs):
        seen = [statrep[q, n + j * pairs + p : n + j * pairs + p + 1, :] for q in range(4) for j in range(2)]
        highs.append(functools.reduce(jnp.maximum, seen))

    def term(p, q, spans):
        for start, size in spans:
            at = at_cols(q, start, size)
            base = n + (pairs if start else 0) + p
            top = statrep[pl.ds(q, 1), base : base + 1, :].reshape(1, samples)
            g_all[at, lanes(p)] = (e_all[p, at, :].astype(F32) * jnp.exp(top - highs[p])).astype(BF16)
        first, size = spans[0][0], sum(x for _, x in spans)
        at = at_cols(q, first, size)
        return lax.dot_general(g_all[at, lanes(p)], weight[at, :], TN, preferred_element_type=F32)

    whole = ((0, cols),)
    wait(e_all.at[:, at_cols(p1), :], r_gc)
    forward(3, *pieces[0], 3)
    for p in range(pairs):
        spans = whole if p < 3 else pieces
        u_acc[lanes(p), :] = term(p, r, spans) + term(p, p1, spans)
    forward(0, 0, cols, 0)
    u_acc[lanes(0), :] += term(0, p2, whole)
    u_acc[lanes(3), :] += term(3, p2, pieces[:1])
    handed(3, *pieces[0], 3)
    u_acc[lanes(3), :] += term(3, p3, pieces[:1])
    handed(0, 0, cols, 0)
    u_acc[lanes(0), :] += term(0, p3, whole)
    forward(1, 0, cols, 1)
    u_acc[lanes(1), :] += term(1, p2, whole)
    wait(statown.at[0 : n - 1], r_so)
    for sp in range(pairs):
        held = statown[:, sp, :]
        pair = []
        for h in range(2):
            s = 2 * sp + h
            rank = rank_all[s * n : (s + 1) * n]
            index = jnp.where(rank >= 0, rank + h * depth, 0)
            value = jnp.where(rank >= 0, lane_pick(held, index), -3.0e38)
            most = jnp.max(value, axis=0, keepdims=True)
            norm = most + jnp.log(jnp.sum(jnp.exp(value - most), axis=0, keepdims=True))
            norms[s : s + 1, :] = norm
            pair.append(
                lane_pick(jnp.broadcast_to(norm, (8, samples)), jnp.broadcast_to(row_index[sp], (8, samples)))[0:1]
            )
        row_norm[sp : sp + 1, :] = jnp.where(lane < depth, pair[0], pair[1])
    scales = []
    for p in range(pairs):
        norm = row_norm[pl.ds(pair_at(p), 1), :]
        valid = row_valid[pl.ds(pair_at(p), 1), :] > 0.5
        scale = jnp.where(valid, jnp.exp(highs[p] - norm), 0.0)
        scales.append(scale)
        s_mat[lanes(p), :] = jnp.transpose(jnp.broadcast_to(scale, (2 * depth, samples)))

    def scaled(values, p):
        return values * jnp.concatenate([s_mat[lanes(p), :]] * (part // samples), axis=1)

    def give_back(p):
        ghsend[lanes(p), :] = (scaled(u_acc[lanes(p), :], p) - t_acc[lanes(p), :]).astype(BF16)
        if p < pairs - 1:
            for h in range(2):
                at = slice((2 * p + h) * depth, (2 * p + h + 1) * depth)
                send(ghsend.at[at], ghrecv.at[at_rows(o)], s_gh, r_gh, 2 * pair_at(p) + h, r)
        else:
            send(ghsend.at[at_rows(2 * p + 1 - y)], ghrecv.at[at_rows(o)], s_gh, r_gh, 2 * z + 1 - y, r)
            ghrecv[at_rows(o), :] = ghsend[at_rows(2 * p + y), :]

    give_back(0)
    handed(1, 0, cols, 1)
    u_acc[lanes(1), :] += term(1, p3, whole)
    give_back(1)
    for sp in range(pairs):
        held = statown[:, pairs + sp, :]
        for h in range(2):
            s = 2 * sp + h
            rank = rank_all[s * n : (s + 1) * n]
            index = jnp.where(rank >= 0, rank + h * depth, 0)
            value = jnp.where(rank >= 0, lane_pick(held, index), 0.0)
            tsums[s : s + 1, :] = jnp.sum(value, axis=0, keepdims=True)
    loss_ref[...] = norms[pl.ds(o, 1), :] - tsums[pl.ds(o, 1), :]
    forward(2, 0, cols, 2)
    u_acc[lanes(2), :] += term(2, p2, whole)
    forward(3, *pieces[1], 4)
    u_acc[lanes(3), :] += term(3, p2, pieces[1:])
    handed(2, 0, cols, 2)
    u_acc[lanes(2), :] += term(2, p3, whole)
    give_back(2)
    handed(3, *pieces[1], 4)
    u_acc[lanes(3), :] += term(3, p3, pieces[1:])
    give_back(3)
    scale_row = jnp.concatenate(scales, axis=1)
    for c in range(4):
        at = slice(c * cols, (c + 1) * cols)
        grad = g_all[at, :].astype(F32) * scale_row - hot[at, :].astype(F32)
        gw_ref[at, :] = jnp.dot(grad.astype(BF16), rows[:, at_part(r)], preferred_element_type=F32).astype(BF16)
    wait(ghrecv.at[0 : (n - 1) * depth], r_gh)
    gh_ref[...] = lax.dot_general(pack, ghrecv[...], TN, preferred_element_type=F32)
    wait(hidden, s_hx)
    wait(metas.at[0 : n - 1], s_meta)
    wait(sendbuf.at[0 : n - 1], s_row)
    wait(sendbuf.at[0 : n - 1], s_rowx)
    wait(wfull.at[:, 0 : 3 * part], s_w)
    wait(rows.at[:, 0 : 2 * part], s_fr)
    wait(statrep.at[0:3], s_sr)
    wait(statown.at[0 : n - 1], s_so)
    for sem in (s_gx, s_gc, s_gr):
        wait(e_all.at[:, 0:cols, :], sem)
    wait(ghsend.at[0 : (n - 1) * depth], s_gh)


def finish(loss_in, gh_in, gw_in, loss_out, gh_out, gw_out, sem):
    moves = [
        pltpu.make_async_copy(a, b, sem.at[i])
        for i, (a, b) in enumerate(((gw_in, gw_out), (gh_in, gh_out), (loss_in, loss_out)))
    ]
    for c in moves:
        c.start()
    for c in moves:
        c.wait()


def fused(hidden, weight, bucket_map, active, label_pick):
    samples, part = hidden.shape
    labels = weight.shape[1]
    n = bucket_map.shape[0]
    depth = 2 * samples * active.shape[1] // n
    cols = labels // 4
    row_count = n * depth
    vmem = pl.BlockSpec(memory_space=pltpu.VMEM)
    hbm = pl.BlockSpec(memory_space=pltpu.HBM)
    dma = pltpu.SemaphoreType.DMA
    sems = [pltpu.SemaphoreType.REGULAR, dma((6,))]
    for received in (None, None, 2, n // 2, n // 2, n // 2, None, None, n // 2 + 1, None, n // 2 + 1, None):
        sems += [dma, dma if received is None else dma((received,))]
    loss, grad_hidden, grad_weight = pl.pallas_call(
        functools.partial(kernel, n, depth),
        out_shape=(
            pltpu.VMEM((1, samples), F32),
            pltpu.VMEM((samples, part), F32),
            pltpu.VMEM((labels, part), BF16),
        ),
        in_specs=[hbm] * 5,
        out_specs=(vmem, vmem, vmem),
        scratch_shapes=[
            pltpu.VMEM((2, samples), jnp.int32),
            pltpu.VMEM((1, samples), jnp.int32),
            pltpu.VMEM((1, n), jnp.int32),
            pltpu.VMEM((8, samples), jnp.int32),
            pltpu.VMEM((samples, part), BF16),
            pltpu.VMEM((samples, part), BF16),
            pltpu.VMEM((labels, part), BF16),
            pltpu.VMEM((n, 8, samples), jnp.int32),
            pltpu.VMEM((cols, 4 * part), BF16),
            pltpu.VMEM((n, depth, part), BF16),
            pltpu.VMEM((n, depth, part), BF16),
            pltpu.VMEM((row_count, 4 * part), BF16),
            pltpu.VMEM((2 * n, samples), F32),
            pltpu.VMEM((4, 2 * n, samples), F32),
            pltpu.VMEM((n, samples), F32),
            pltpu.VMEM((n, n, samples), F32),
            pltpu.VMEM((n, samples), F32),
            pltpu.VMEM((n, samples), F32),
            pltpu.VMEM((8, samples), jnp.int32),
            pltpu.VMEM((8, samples), F32),
            pltpu.VMEM((8, samples), F32),
            pltpu.VMEM((n // 2, labels, 2 * depth), BF16),
            pltpu.VMEM((labels, row_count), BF16),
            pltpu.VMEM((labels, row_count), BF16),
            pltpu.VMEM((row_count, part), F32),
            pltpu.VMEM((row_count, part), F32),
            pltpu.VMEM((row_count, samples), F32),
            pltpu.VMEM((row_count, part), BF16),
            pltpu.VMEM((row_count, part), BF16),
        ] + sems,
        compiler_params=pltpu.CompilerParams(
            collective_id=0, has_side_effects=True, vmem_limit_bytes=60 * 1024 * 1024
        ),
    )(active.T, label_pick[None], bucket_map[None], hidden, weight[0])
    loss, grad_hidden, grad_weight = pl.pallas_call(
        finish,
        out_shape=(
            jax.ShapeDtypeStruct((1, samples), F32),
            jax.ShapeDtypeStruct((samples, part), F32),
            jax.ShapeDtypeStruct((labels, part), BF16),
        ),
        in_specs=[vmem] * 3,
        out_specs=(hbm, hbm, hbm),
        scratch_shapes=[dma((3,))],
        compiler_params=pltpu.CompilerParams(vmem_limit_bytes=1024 * 1024),
    )(loss, grad_hidden, grad_weight)
    return loss[0], grad_hidden, grad_weight[None]


def body(hidden, weight, bucket_map, active, label_pick):
    samp_count = hidden.shape[0]
    bucket_dev, label_count, feature_part = weight.shape
    picks = active.shape[1]
    bucket_total = bucket_map.shape[0]
    owner_count = lax.axis_size("own")
    slot_depth = max(2, 2 * samp_count * picks // bucket_total)
    pair_count = samp_count * picks
    slots_total = bucket_total * slot_depth
    row_count = owner_count * slot_depth
    pair_bucket = active.reshape(pair_count)
    bucket_iota = lax.broadcasted_iota(jnp.int32, (pair_count, bucket_total), 1)
    slot_index = jnp.sum(
        jnp.where(pair_bucket[:, None] == bucket_iota, bucket_map[None, :], 0), axis=1
    )
    slot_hits = (slot_index[:, None] == bucket_iota).astype(jnp.int32)
    before = lax.broadcasted_iota(jnp.int32, (pair_count, pair_count), 0)
    after = lax.broadcasted_iota(jnp.int32, (pair_count, pair_count), 1)
    earlier = jnp.dot(
        (after < before).astype(BF16), slot_hits.astype(BF16), preferred_element_type=F32
    ).astype(jnp.int32)
    rank_within = jnp.sum(earlier * slot_hits, axis=1)
    position = slot_index * slot_depth + rank_within
    pair_index = jnp.arange(pair_count, dtype=jnp.int32)
    pick_value = jnp.repeat(label_pick, picks)
    target_pair = jnp.where(
        pick_value // label_count == pair_index % picks, pick_value % label_count, -1
    )
    width_sent = hidden.shape[1]
    pair_rows = jnp.repeat(hidden, picks, axis=0)
    send_rows = jnp.zeros((slots_total, width_sent), jnp.bfloat16).at[position].set(pair_rows)
    send_target = jnp.full((slots_total,), -1, jnp.int32).at[position].set(target_pair)
    got_rows, got_target = (
        lax.all_to_all(
            send_rows.reshape(owner_count, bucket_dev * slot_depth, width_sent),
            "own",
            split_axis=0,
            concat_axis=0,
            tiled=True,
        ),
        lax.all_to_all(
            send_target.reshape(owner_count, bucket_dev * slot_depth),
            "own",
            split_axis=0,
            concat_axis=0,
            tiled=True,
        ),
    )
    received = got_rows.reshape(owner_count, bucket_dev, slot_depth, width_sent).transpose(
        1, 0, 2, 3
    )
    received = received.reshape(bucket_dev, row_count, width_sent)
    target_col = (
        got_target.reshape(owner_count, bucket_dev, slot_depth)
        .transpose(1, 0, 2)
        .reshape(bucket_dev, row_count)
    )
    partial_value = jnp.einsum("brd,bcd->brc", received, weight, preferred_element_type=jnp.float32)
    logits = lax.psum(partial_value, "rep")
    columns = lax.broadcasted_iota(jnp.int32, (1, 1, label_count), 2)
    row_max = jnp.max(logits, axis=2)
    row_sum = jnp.sum(jnp.exp(logits - row_max[..., None]), axis=2)
    row_target = jnp.sum(jnp.where(columns == target_col[..., None], logits, 0.0), axis=2)

    def to_sources(values):
        return (
            values.reshape(bucket_dev, owner_count, slot_depth)
            .transpose(1, 0, 2)
            .reshape(owner_count, bucket_dev * slot_depth)
        )

    back_max, back_sum, back_target = (
        lax.all_to_all(to_sources(row_max), "own", split_axis=0, concat_axis=0, tiled=True),
        lax.all_to_all(to_sources(row_sum), "own", split_axis=0, concat_axis=0, tiled=True),
        lax.all_to_all(to_sources(row_target), "own", split_axis=0, concat_axis=0, tiled=True),
    )
    pair_max = back_max.reshape(slots_total)[position].reshape(samp_count, picks)
    pair_sum = back_sum.reshape(slots_total)[position].reshape(samp_count, picks)
    pair_target = back_target.reshape(slots_total)[position].reshape(samp_count, picks)
    peak_max = jnp.max(pair_max, axis=1)
    norm_sum = jnp.sum(pair_sum * jnp.exp(pair_max - peak_max[:, None]), axis=1)
    log_norm = peak_max + jnp.log(norm_sum)
    sample_loss = log_norm - jnp.sum(pair_target, axis=1)
    send_norm = jnp.zeros((slots_total,), jnp.float32).at[position].set(jnp.repeat(log_norm, picks))
    got_norm = lax.all_to_all(
        send_norm.reshape(owner_count, bucket_dev * slot_depth),
        "own",
        split_axis=0,
        concat_axis=0,
        tiled=True,
    )
    row_norm = (
        got_norm.reshape(owner_count, bucket_dev, slot_depth)
        .transpose(1, 0, 2)
        .reshape(bucket_dev, row_count)
    )
    onehot = (columns == target_col[..., None]).astype(jnp.float32)
    grad_logits = (jnp.exp(logits - row_norm[..., None]) - onehot).astype(jnp.bfloat16)
    grad_weight = jnp.einsum(
        "brc,brd->bcd", grad_logits, received, preferred_element_type=jnp.float32
    ).astype(jnp.bfloat16)
    row_grads = jnp.einsum("brc,bcd->brd", grad_logits, weight, preferred_element_type=jnp.float32)
    send_grads = row_grads.reshape(bucket_dev, owner_count, slot_depth, feature_part).transpose(
        1, 0, 2, 3
    )
    send_grads = send_grads.reshape(owner_count, bucket_dev * slot_depth, feature_part)
    got_grads = lax.all_to_all(send_grads, "own", split_axis=0, concat_axis=0, tiled=True)
    pair_grads = got_grads.reshape(slots_total, feature_part)[position].reshape(
        samp_count, picks, feature_part
    )
    grad_hidden = jnp.sum(pair_grads, axis=1)
    return (sample_loss, grad_hidden, grad_weight)


def choose(hidden, weight, bucket_map, active, label_pick):
    samples, picks = active.shape
    buckets = bucket_map.shape[0]
    depth = 2 * samples * picks // buckets
    fits = (
        weight.shape[0] == 1
        and lax.axis_size("rep") == 4
        and buckets == 8
        and picks == 2
        and samples == 128
        and 2 * depth == samples
        and weight.shape[1] % 512 == 0
        and hidden.shape[1] % 128 == 0
    )
    run = fused if fits else body
    return run(hidden, weight, bucket_map, active, label_pick)


def solution(mesh):
    in_specs = (P("own", "rep"), P("own", None, "rep"), P(), P("own", None), P("own"))
    out_specs = (P("own"), P("own", "rep"), P("own", None, "rep"))
    return jax.shard_map(choose, mesh=mesh, in_specs=in_specs, out_specs=out_specs, check_vma=False)
```

```python
import functools
import jax
import jax.numpy as jnp
from jax import lax
from jax.experimental import pallas as pl
from jax.experimental.pallas import tpu as pltpu
from jax.sharding import PartitionSpec as P

MESH = pl.DeviceIdType.MESH
F32 = jnp.float32
BF16 = jnp.bfloat16
NT = (((1,), (1,)), ((), ()))
TN = (((0,), (0,)), ((), ()))


def ranks(slot0, slot1, buckets, upper):
    sources, samples = slot0.shape
    bucket = lax.broadcasted_iota(jnp.int32, (buckets, samples), 0)
    hits = [
        jnp.where((slot0[s : s + 1] == bucket) | (slot1[s : s + 1] == bucket), 1.0, 0.0)
        for s in range(sources)
    ]
    hits = jnp.concatenate(hits, axis=0) if sources > 1 else hits[0]
    earlier = jnp.dot(hits.astype(BF16), upper, preferred_element_type=F32)
    return jnp.where(hits > 0.5, earlier, -1.0).astype(jnp.int32)


def lane_pick(values, index):
    return jnp.take_along_axis(values, index, axis=1)


def kernel(
    n, depth, act_hbm, pick_hbm, map_hbm, hidden_hbm, weight_hbm,
    loss_ref, gh_ref, gw_ref,
    act, pick_own, table_in, meta, hidden, hidden_x, weight, metas, wfull, sendbuf, sendbuf_x, rows, stats, statrep, comb, statown,
    norms, tsums, row_target, row_valid, row_norm, e_all, g_all, hot, u_acc, t_acc, s_mat, ghsend, ghrecv,
    go, s_loc, s_hx, r_hx, s_meta, r_meta, s_w, r_w, s_row, r_row, s_rowx, r_rowx, s_fr, r_fr,
    s_sr, r_sr, s_so, r_so, s_gx, r_gx, s_gc, r_gc, s_gr, r_gr, s_gh, r_gh,
):
    labels, part = weight_hbm.shape
    samples = hidden_hbm.shape[0]
    cols = labels // 4
    pairs = n // 2
    o = lax.axis_index("own")
    r = lax.axis_index("rep")
    z = o // 2
    y = o - 2 * z
    p1 = r + 1 - 2 * lax.rem(r, 2)
    p2 = lax.rem(r + 2, 4)
    p3 = lax.rem(p1 + 2, 4)
    row_count = n * depth
    local = [
        pltpu.make_async_copy(act_hbm, act, s_loc.at[0]),
        pltpu.make_async_copy(hidden_hbm, hidden, s_loc.at[1]),
        pltpu.make_async_copy(weight_hbm, weight, s_loc.at[2]),
        pltpu.make_async_copy(
            weight_hbm.at[pl.ds(pl.multiple_of(r * cols, cols), cols)],
            wfull.at[:, pl.ds(pl.multiple_of(r * part, part), part)],
            s_loc.at[3],
        ),
        pltpu.make_async_copy(pick_hbm, pick_own, s_loc.at[4]),
        pltpu.make_async_copy(map_hbm, table_in, s_loc.at[5]),
    ]

    def send(src, dst, ssem, rsem, own, rep):
        copy = pltpu.make_async_remote_copy(
            src_ref=src, dst_ref=dst, send_sem=ssem, recv_sem=rsem,
            device_id={"own": own, "rep": rep}, device_id_type=MESH,
        )
        copy.start()

    def wait(ref, sem):
        pltpu.make_async_copy(ref, ref, sem).wait()

    peers = []
    for turned in (pairs - 1 - z, lax.rem(z + 2, pairs), z + 1 - 2 * lax.rem(z, 2)):
        peers += [2 * turned, 2 * turned + 1]
    peers.append(2 * z + 1 - y)

    def at_rows(s):
        return pl.ds(pl.multiple_of(s * depth, depth), depth)

    def turn_of(to):
        return lax.rem(z - to // 2 + pairs + pairs - 1, pairs)

    def pair_at(p):
        return lax.rem(z + 1 + p, pairs)

    def at_part(q):
        return pl.ds(pl.multiple_of(q * part, part), part)

    unit = cols // 4
    pieces = ((0, cols - unit), (cols - unit, unit))

    def at_cols(q, start=0, size=None):
        size = cols if size is None else size
        return pl.ds(pl.multiple_of(q * cols + start, unit), size)

    def lanes(p):
        return slice(p * 2 * depth, (p + 1) * 2 * depth)

    barrier = pltpu.get_barrier_semaphore()
    odd = lax.rem(r, 2)
    even = r - odd

    def greet(own, rep):
        pl.semaphore_signal(barrier, inc=1, device_id={"own": own, "rep": rep}, device_id_type=MESH)

    @pl.when(odd == 0)
    def _():
        greet(o, p2)
        greet(o, p1)

    @pl.when(odd == 1)
    def _():
        greet(o, p1)
        greet(o, p3)

    for to in peers:
        greet(to, even + 1)
    for c in local:
        c.start()

    @pl.when(odd == 0)
    def _():
        pl.semaphore_wait(barrier, 3)
        pl.semaphore_signal(go, inc=1, device_id={"own": o, "rep": p1}, device_id_type=MESH)

    @pl.when(odd == 1)
    def _():
        pl.semaphore_wait(go, 1)

    send(hidden_hbm, hidden_x, s_hx, r_hx, o, p2)
    for j, (start, size) in enumerate(pieces):
        for q in (p2, p3, p1):
            send(weight_hbm.at[at_cols(q, start, size)], wfull.at[start : start + size, at_part(r)], s_w, r_w.at[j], o, q)
    local[0].wait()
    local[4].wait()
    local[5].wait()
    meta[0:2, :] = act[...]
    meta[2:3, :] = pick_own[...]
    meta[3:8, :] = jnp.zeros((5, samples), jnp.int32)
    meta[3:4, 0:n] = table_in[...]
    local[1].wait()
    below = lax.broadcasted_iota(jnp.int32, (samples, samples), 0)
    right = lax.broadcasted_iota(jnp.int32, (samples, samples), 1)
    upper = jnp.where(below < right, 1.0, 0.0).astype(BF16)

    def slots(ids):
        table = jnp.broadcast_to(meta[3:4, :], (n, samples))
        return lane_pick(table, jnp.broadcast_to(ids, (n, samples)))[: ids.shape[0]]

    mine = meta[...]
    own_rank = ranks(slots(mine[0:1]), slots(mine[1:2]), n, upper)
    place = lax.broadcasted_iota(jnp.int32, (depth, samples), 0)
    pack = jnp.concatenate(
        [jnp.where(own_rank[b : b + 1] == place, 1.0, 0.0).astype(BF16) for b in range(n)], axis=0
    )
    packed = jnp.dot(pack, hidden[...], preferred_element_type=F32).astype(BF16)
    for b in range(n):
        sendbuf[b] = packed[b * depth : (b + 1) * depth]

    @pl.when(odd == 1)
    def _():
        pl.semaphore_wait(barrier, 2 * (n - 1) + 1)
        pl.semaphore_signal(go, inc=1, device_id={"own": o, "rep": p1}, device_id_type=MESH)

    @pl.when(odd == 0)
    def _():
        pl.semaphore_wait(go, 1)

    for to in peers:
        send(meta, metas.at[o], s_meta, r_meta, to, r)
    row_order = peers[6:7] + peers[4:6] + peers[0:2] + peers[2:4]
    rowx_order = peers[6:7] + peers[4:6] + peers[0:2] + peers[2:4]
    for to in row_order:
        p = turn_of(to)
        send(sendbuf.at[to], rows.at[at_rows(2 * p + y), at_part(r)], s_row, r_row.at[p], to, r)
    own_rows = at_rows(2 * (pairs - 1) + y)
    rows[own_rows, at_part(r)] = sendbuf[o]
    metas[o] = mine

    wait(hidden_x, r_hx)
    packed_x = jnp.dot(pack, hidden_x[...], preferred_element_type=F32).astype(BF16)
    for b in range(n):
        sendbuf_x[b] = packed_x[b * depth : (b + 1) * depth]
    for to in rowx_order:
        p = turn_of(to)
        send(sendbuf_x.at[to], rows.at[at_rows(2 * p + y), at_part(p2)], s_rowx, r_rowx.at[p], to, r)
    rows[own_rows, at_part(p2)] = sendbuf_x[o]

    wait(metas.at[0 : n - 1], r_meta)
    slot0 = slots(metas[:, 0, :])
    slot1 = slots(metas[:, 1, :])
    pick = metas[:, 2, :]
    rank_all = ranks(slot0, slot1, n, upper)
    wanted = jnp.where(pick < labels, slot0, slot1)
    code = jnp.where(wanted == o, jnp.where(pick < labels, pick, pick - labels) + 1, 0)
    code_hi = (code // 64).astype(F32)
    code_lo = (code - (code // 64) * 64).astype(F32)
    lane = lax.broadcasted_iota(jnp.int32, (1, samples), 1)
    sub = lax.broadcasted_iota(jnp.int32, (8, samples), 0)
    bucket_sub = lax.broadcasted_iota(jnp.int32, (n, samples), 0)
    row_index = []
    place2 = lax.broadcasted_iota(jnp.int32, (2 * depth, samples), 0)
    for sp in range(pairs):
        info = jnp.zeros((8, 2 * depth), F32)
        for h in range(2):
            s = 2 * sp + h
            rank_me = jnp.max(
                jnp.where(bucket_sub == o, rank_all[s * n : (s + 1) * n], -1), axis=0, keepdims=True
            )
            member = jnp.where(
                (rank_me >= 0) & (rank_me + h * depth == place2), 1.0, 0.0
            ).astype(BF16)
            facts = jnp.where(
                sub == 0, lane.astype(F32),
                jnp.where(sub == 1, code_hi[s : s + 1], jnp.where(sub == 2, code_lo[s : s + 1], jnp.where(sub == 3, 1.0, 0.0))),
            ).astype(BF16)
            info = info + lax.dot_general(facts, member, NT, preferred_element_type=F32)
        row_index.append(info[0:1].astype(jnp.int32))
        row_valid[sp : sp + 1, :] = info[3:4]
        row_target[sp : sp + 1, :] = (info[1:2] * 64.0 + info[2:3]).astype(jnp.int32) - 1
    targets_at = [row_target[pl.ds(pair_at(p), 1), :] for p in range(pairs)]
    target_row = jnp.concatenate(targets_at, axis=1)

    def hand_over(p, q, sem):
        got = lanes(p) if p < pairs - 1 else at_rows(2 * p + 1 - y)
        wait(rows.at[got, at_part(q)], sem.at[p])
        block = rows.at[lanes(p), at_part(q)]
        send(block, block, s_fr, r_fr.at[p], o, p1)

    hand_over(3, r, r_row)
    hand_over(3, p2, r_rowx)
    local[2].wait()
    local[3].wait()
    for c in range(4):
        at = slice(c * cols, (c + 1) * cols)
        ids = lax.broadcasted_iota(jnp.int32, (cols, row_count), 0) + c * cols
        hot[at, :] = jnp.where(ids == target_row, 1.0, 0.0).astype(BF16)
    for p in range(pairs):
        t_acc[lanes(p), :] = lax.dot_general(hot[:, lanes(p)], weight[...], TN, preferred_element_type=F32)
    for p in range(3):
        hand_over(p, r, r_row)

    def pass_x(p, start, size, turn):
        block = e_all.at[p, at_cols(r, start, size), :]
        send(block, block, s_gx, r_gx.at[turn], o, p2)

    def pass_c(p, start, size):
        block = e_all.at[p, at_cols(r, start, size), :]
        send(block, block, s_gc, r_gc, o, p1)

    def scores(first, last, start, size):
        at = slice(first * 2 * depth, last * 2 * depth)
        width = (last - first) * 2 * depth
        logits = lax.dot_general(wfull[start : start + size, :], rows[at, :], NT, preferred_element_type=F32)
        top = jnp.max(logits, axis=0, keepdims=True)
        raised = jnp.exp(logits - top)
        for p in range(first, last):
            e_all[p, at_cols(r, start, size), :] = raised[:, (p - first) * 2 * depth : (p - first + 1) * 2 * depth].astype(BF16)
        if first in (0, 3) and start == 0:
            pass_x(first, start, size, first)
        label_id = lax.broadcasted_iota(jnp.int32, (size, width), 0) + (r * cols + start)
        target = jnp.sum(jnp.where(label_id == target_row[:, at], logits, 0.0), axis=0, keepdims=True)
        return top, jnp.sum(raised, axis=0, keepdims=True), target

    for j, (start, size) in enumerate(pieces):
        wait(wfull.at[start : start + size, 0 : 3 * part], r_w.at[j])
        if j == 0:
            wait(rows.at[lanes(3), 0 : 2 * part], r_fr.at[3])
            top_d, sum_d, target_d = scores(3, 4, start, size)
            pass_c(3, start, size)
            hand_over(0, p2, r_rowx)
            hand_over(2, p2, r_rowx)
            wait(rows.at[lanes(0), 0 : 2 * part], r_fr.at[0])
            top_a, sum_a, target_a = scores(0, 1, start, size)
            hand_over(1, p2, r_rowx)
        else:
            wait(rows.at[lanes(1), 0 : 2 * part], r_fr.at[1])
            wait(rows.at[lanes(2), 0 : 2 * part], r_fr.at[2])
            top_r, sum_r, target_r = scores(1, 3, 0, cols)
            top_b, sum_b, target_b = scores(0, 1, start, size)
            top_e, sum_e, target_e = scores(3, 4, start, size)

    def merged(top0, sum0, top1, sum1):
        peak = jnp.maximum(top0, top1)
        return peak + jnp.log(sum0 * jnp.exp(top0 - peak) + sum1 * jnp.exp(top1 - peak))

    lse = jnp.concatenate(
        [merged(top_a, sum_a, top_b, sum_b), top_r + jnp.log(sum_r), merged(top_d, sum_d, top_e, sum_e)], axis=1
    )
    target_sum = jnp.concatenate([target_a + target_b, target_r, target_d + target_e], axis=1)
    tops = [jnp.concatenate([top_a, top_r, top_d], axis=1), jnp.concatenate([top_b, top_r, top_e], axis=1)]
    for p in range(pairs):
        stats[p : p + 1, :] = lse[:, lanes(p)]
        stats[pairs + p : pairs + p + 1, :] = target_sum[:, lanes(p)]
        stats[n + p : n + p + 1, :] = tops[0][:, lanes(p)]
        stats[n + pairs + p : n + pairs + p + 1, :] = tops[1][:, lanes(p)]
    for q in (p2, p3, p1):
        send(stats, statrep.at[r], s_sr, r_sr, o, q)
    pass_x(0, *pieces[1], 0)
    pass_x(1, 0, cols, 1)
    pass_c(2, 0, cols)
    pass_c(3, *pieces[1])
    for p in range(2):
        pass_c(p, 0, cols)
    statrep[r] = stats[...]
    wait(statrep.at[0:3], r_sr)
    parts = [statrep[q, 0:n, :] for q in range(4)]
    high = jnp.maximum(jnp.maximum(parts[0], parts[1]), jnp.maximum(parts[2], parts[3]))
    total = high + jnp.log(sum(jnp.exp(x - high) for x in parts))
    summed = sum(parts)
    for p in range(pairs):
        comb[pl.ds(pair_at(p), 1), :] = total[p : p + 1]
        comb[pl.ds(pairs + pair_at(p), 1), :] = summed[pairs + p : pairs + p + 1]
    for to in peers:
        send(comb, statown.at[o], s_so, r_so, to, r)
    statown[o] = comb[...]

    def forward(p, start, size, turn):
        block = e_all.at[p, at_cols(p2, start, size), :]
        wait(block, r_gx.at[turn])
        send(block, block, s_gr, r_gr.at[turn], o, p1)

    def handed(p, start, size, turn):
        wait(e_all.at[p, at_cols(p3, start, size), :], r_gr.at[turn])

    highs = []
    for p in range(pairs):
        seen = [statrep[q, n + j * pairs + p : n + j * pairs + p + 1, :] for q in range(4) for j in range(2)]
        highs.append(functools.reduce(jnp.maximum, seen))

    def term(p, q, spans):
        for start, size in spans:
            at = at_cols(q, start, size)
            base = n + (pairs if start else 0) + p
            top = statrep[pl.ds(q, 1), base : base + 1, :].reshape(1, samples)
            g_all[at, lanes(p)] = (e_all[p, at, :].astype(F32) * jnp.exp(top - highs[p])).astype(BF16)
        first, size = spans[0][0], sum(x for _, x in spans)
        at = at_cols(q, first, size)
        return lax.dot_general(g_all[at, lanes(p)], weight[at, :], TN, preferred_element_type=F32)

    whole = ((0, cols),)
    late = ((2, 0, cols, 2), (3, *pieces[1], 4))
    wait(e_all.at[:, at_cols(p1), :], r_gc)

    @pl.when(odd == 1)
    def _():
        for p, start, size, turn in late:
            for q, to in ((p1, p3), (r, p2)):
                block = e_all.at[p, at_cols(q, start, size), :]
                send(block, block, s_gx, r_gx.at[turn], o, to)

    forward(3, *pieces[0], 3)
    for p in range(pairs):
        spans = whole if p in (1, 2) else pieces
        u_acc[lanes(p), :] = term(p, r, spans) + term(p, p1, spans)
    forward(0, 0, cols, 0)
    u_acc[lanes(0), :] += term(0, p2, pieces)
    u_acc[lanes(3), :] += term(3, p2, pieces[:1])
    handed(3, *pieces[0], 3)
    u_acc[lanes(3), :] += term(3, p3, pieces[:1])
    handed(0, 0, cols, 0)
    u_acc[lanes(0), :] += term(0, p3, pieces)
    forward(1, 0, cols, 1)
    u_acc[lanes(1), :] += term(1, p2, whole)
    wait(statown.at[0 : n - 1], r_so)
    for sp in range(pairs):
        held = statown[:, sp, :]
        pair = []
        for h in range(2):
            s = 2 * sp + h
            rank = rank_all[s * n : (s + 1) * n]
            index = jnp.where(rank >= 0, rank + h * depth, 0)
            value = jnp.where(rank >= 0, lane_pick(held, index), -3.0e38)
            most = jnp.max(value, axis=0, keepdims=True)
            norm = most + jnp.log(jnp.sum(jnp.exp(value - most), axis=0, keepdims=True))
            norms[s : s + 1, :] = norm
            pair.append(
                lane_pick(jnp.broadcast_to(norm, (8, samples)), jnp.broadcast_to(row_index[sp], (8, samples)))[0:1]
            )
        row_norm[sp : sp + 1, :] = jnp.where(lane < depth, pair[0], pair[1])
    scales = []
    for p in range(pairs):
        norm = row_norm[pl.ds(pair_at(p), 1), :]
        valid = row_valid[pl.ds(pair_at(p), 1), :] > 0.5
        scale = jnp.where(valid, jnp.exp(highs[p] - norm), 0.0)
        scales.append(scale)
        s_mat[lanes(p), :] = jnp.transpose(jnp.broadcast_to(scale, (2 * depth, samples)))

    def scaled(values, p):
        return values * jnp.concatenate([s_mat[lanes(p), :]] * (part // samples), axis=1)

    def give_back(p):
        ghsend[lanes(p), :] = (scaled(u_acc[lanes(p), :], p) - t_acc[lanes(p), :]).astype(BF16)
        if p < pairs - 1:
            for h in range(2):
                at = slice((2 * p + h) * depth, (2 * p + h + 1) * depth)
                send(ghsend.at[at], ghrecv.at[at_rows(o)], s_gh, r_gh, 2 * pair_at(p) + h, r)
        else:
            send(ghsend.at[at_rows(2 * p + 1 - y)], ghrecv.at[at_rows(o)], s_gh, r_gh, 2 * z + 1 - y, r)
            ghrecv[at_rows(o), :] = ghsend[at_rows(2 * p + y), :]

    give_back(0)
    handed(1, 0, cols, 1)
    u_acc[lanes(1), :] += term(1, p3, whole)
    give_back(1)
    forward(2, 0, cols, 2)
    u_acc[lanes(2), :] += term(2, p2, whole)
    forward(3, *pieces[1], 4)
    u_acc[lanes(3), :] += term(3, p2, pieces[1:])
    handed(2, 0, cols, 2)
    u_acc[lanes(2), :] += term(2, p3, whole)
    give_back(2)
    handed(3, *pieces[1], 4)
    u_acc[lanes(3), :] += term(3, p3, pieces[1:])
    give_back(3)
    scale_row = jnp.concatenate(scales, axis=1)
    for c in range(4):
        at = slice(c * cols, (c + 1) * cols)
        grad = g_all[at, :].astype(F32) * scale_row - hot[at, :].astype(F32)
        gw_ref[at, :] = jnp.dot(grad.astype(BF16), rows[:, at_part(r)], preferred_element_type=F32).astype(BF16)
    for sp in range(pairs):
        held = statown[:, pairs + sp, :]
        for h in range(2):
            s = 2 * sp + h
            rank = rank_all[s * n : (s + 1) * n]
            index = jnp.where(rank >= 0, rank + h * depth, 0)
            value = jnp.where(rank >= 0, lane_pick(held, index), 0.0)
            tsums[s : s + 1, :] = jnp.sum(value, axis=0, keepdims=True)
    loss_ref[...] = norms[pl.ds(o, 1), :] - tsums[pl.ds(o, 1), :]
    wait(ghrecv.at[0 : (n - 1) * depth], r_gh)
    gh_ref[...] = lax.dot_general(pack, ghrecv[...], TN, preferred_element_type=F32)
    wait(hidden, s_hx)
    wait(metas.at[0 : n - 1], s_meta)
    wait(sendbuf.at[0 : n - 1], s_row)
    wait(sendbuf.at[0 : n - 1], s_rowx)
    wait(wfull.at[:, 0 : 3 * part], s_w)
    wait(rows.at[:, 0 : 2 * part], s_fr)
    wait(statrep.at[0:3], s_sr)
    wait(statown.at[0 : n - 1], s_so)
    early_bytes = (2 * cols + pieces[0][1]) // pairs
    late_bytes = 2 * (cols + pieces[1][1]) // pairs

    @pl.when(odd == 0)
    def _():
        wait(hot.at[0:early_bytes], s_gx)

    @pl.when(odd == 1)
    def _():
        wait(hot.at[0 : early_bytes + late_bytes], s_gx)

    for sem in (s_gc, s_gr):
        wait(e_all.at[:, 0:cols, :], sem)
    wait(ghsend.at[0 : (n - 1) * depth], s_gh)


def finish(loss_in, gh_in, gw_in, loss_out, gh_out, gw_out, sem):
    step = gw_in.shape[0] // 4
    cuts = [pl.ds(i * step, step) for i in range(4)]
    pairs = [(gw_in.at[at], gw_out.at[at]) for at in cuts] + [(gh_in, gh_out), (loss_in, loss_out)]
    moves = [
        pltpu.make_async_copy(a, b, sem.at[i])
        for i, (a, b) in enumerate(pairs)
    ]
    for c in moves:
        c.start()
    for c in moves:
        c.wait()


def fused(hidden, weight, bucket_map, active, label_pick):
    samples, part = hidden.shape
    labels = weight.shape[1]
    n = bucket_map.shape[0]
    depth = 2 * samples * active.shape[1] // n
    cols = labels // 4
    row_count = n * depth
    vmem = pl.BlockSpec(memory_space=pltpu.VMEM)
    hbm = pl.BlockSpec(memory_space=pltpu.HBM)
    dma = pltpu.SemaphoreType.DMA
    sems = [pltpu.SemaphoreType.REGULAR, dma((6,))]
    for received in (None, None, 2, n // 2, n // 2, n // 2, None, None, n // 2 + 1, None, n // 2 + 1, None):
        sems += [dma, dma if received is None else dma((received,))]
    loss, grad_hidden, grad_weight = pl.pallas_call(
        functools.partial(kernel, n, depth),
        out_shape=(
            pltpu.VMEM((1, samples), F32),
            pltpu.VMEM((samples, part), F32),
            pltpu.VMEM((labels, part), BF16),
        ),
        in_specs=[hbm] * 5,
        out_specs=(vmem, vmem, vmem),
        scratch_shapes=[
            pltpu.VMEM((2, samples), jnp.int32),
            pltpu.VMEM((1, samples), jnp.int32),
            pltpu.VMEM((1, n), jnp.int32),
            pltpu.VMEM((8, samples), jnp.int32),
            pltpu.VMEM((samples, part), BF16),
            pltpu.VMEM((samples, part), BF16),
            pltpu.VMEM((labels, part), BF16),
            pltpu.VMEM((n, 8, samples), jnp.int32),
            pltpu.VMEM((cols, 4 * part), BF16),
            pltpu.VMEM((n, depth, part), BF16),
            pltpu.VMEM((n, depth, part), BF16),
            pltpu.VMEM((row_count, 4 * part), BF16),
            pltpu.VMEM((2 * n, samples), F32),
            pltpu.VMEM((4, 2 * n, samples), F32),
            pltpu.VMEM((n, samples), F32),
            pltpu.VMEM((n, n, samples), F32),
            pltpu.VMEM((n, samples), F32),
            pltpu.VMEM((n, samples), F32),
            pltpu.VMEM((8, samples), jnp.int32),
            pltpu.VMEM((8, samples), F32),
            pltpu.VMEM((8, samples), F32),
            pltpu.VMEM((n // 2, labels, 2 * depth), BF16),
            pltpu.VMEM((labels, row_count), BF16),
            pltpu.VMEM((labels, row_count), BF16),
            pltpu.VMEM((row_count, part), F32),
            pltpu.VMEM((row_count, part), F32),
            pltpu.VMEM((row_count, samples), F32),
            pltpu.VMEM((row_count, part), BF16),
            pltpu.VMEM((row_count, part), BF16),
        ] + sems,
        compiler_params=pltpu.CompilerParams(
            collective_id=0, has_side_effects=True, vmem_limit_bytes=60 * 1024 * 1024
        ),
    )(active.T, label_pick[None], bucket_map[None], hidden, weight[0])
    loss, grad_hidden, grad_weight = pl.pallas_call(
        finish,
        out_shape=(
            jax.ShapeDtypeStruct((1, samples), F32),
            jax.ShapeDtypeStruct((samples, part), F32),
            jax.ShapeDtypeStruct((labels, part), BF16),
        ),
        in_specs=[vmem] * 3,
        out_specs=(hbm, hbm, hbm),
        scratch_shapes=[dma((6,))],
        compiler_params=pltpu.CompilerParams(vmem_limit_bytes=1024 * 1024),
    )(loss, grad_hidden, grad_weight)
    return loss[0], grad_hidden, grad_weight[None]


def body(hidden, weight, bucket_map, active, label_pick):
    samp_count = hidden.shape[0]
    bucket_dev, label_count, feature_part = weight.shape
    picks = active.shape[1]
    bucket_total = bucket_map.shape[0]
    owner_count = lax.axis_size("own")
    slot_depth = max(2, 2 * samp_count * picks // bucket_total)
    pair_count = samp_count * picks
    slots_total = bucket_total * slot_depth
    row_count = owner_count * slot_depth
    pair_bucket = active.reshape(pair_count)
    bucket_iota = lax.broadcasted_iota(jnp.int32, (pair_count, bucket_total), 1)
    slot_index = jnp.sum(
        jnp.where(pair_bucket[:, None] == bucket_iota, bucket_map[None, :], 0), axis=1
    )
    slot_hits = (slot_index[:, None] == bucket_iota).astype(jnp.int32)
    before = lax.broadcasted_iota(jnp.int32, (pair_count, pair_count), 0)
    after = lax.broadcasted_iota(jnp.int32, (pair_count, pair_count), 1)
    earlier = jnp.dot(
        (after < before).astype(BF16), slot_hits.astype(BF16), preferred_element_type=F32
    ).astype(jnp.int32)
    rank_within = jnp.sum(earlier * slot_hits, axis=1)
    position = slot_index * slot_depth + rank_within
    pair_index = jnp.arange(pair_count, dtype=jnp.int32)
    pick_value = jnp.repeat(label_pick, picks)
    target_pair = jnp.where(
        pick_value // label_count == pair_index % picks, pick_value % label_count, -1
    )
    width_sent = hidden.shape[1]
    pair_rows = jnp.repeat(hidden, picks, axis=0)
    send_rows = jnp.zeros((slots_total, width_sent), jnp.bfloat16).at[position].set(pair_rows)
    send_target = jnp.full((slots_total,), -1, jnp.int32).at[position].set(target_pair)
    got_rows, got_target = (
        lax.all_to_all(
            send_rows.reshape(owner_count, bucket_dev * slot_depth, width_sent),
            "own",
            split_axis=0,
            concat_axis=0,
            tiled=True,
        ),
        lax.all_to_all(
            send_target.reshape(owner_count, bucket_dev * slot_depth),
            "own",
            split_axis=0,
            concat_axis=0,
            tiled=True,
        ),
    )
    received = got_rows.reshape(owner_count, bucket_dev, slot_depth, width_sent).transpose(
        1, 0, 2, 3
    )
    received = received.reshape(bucket_dev, row_count, width_sent)
    target_col = (
        got_target.reshape(owner_count, bucket_dev, slot_depth)
        .transpose(1, 0, 2)
        .reshape(bucket_dev, row_count)
    )
    partial_value = jnp.einsum("brd,bcd->brc", received, weight, preferred_element_type=jnp.float32)
    logits = lax.psum(partial_value, "rep")
    columns = lax.broadcasted_iota(jnp.int32, (1, 1, label_count), 2)
    row_max = jnp.max(logits, axis=2)
    row_sum = jnp.sum(jnp.exp(logits - row_max[..., None]), axis=2)
    row_target = jnp.sum(jnp.where(columns == target_col[..., None], logits, 0.0), axis=2)

    def to_sources(values):
        return (
            values.reshape(bucket_dev, owner_count, slot_depth)
            .transpose(1, 0, 2)
            .reshape(owner_count, bucket_dev * slot_depth)
        )

    back_max, back_sum, back_target = (
        lax.all_to_all(to_sources(row_max), "own", split_axis=0, concat_axis=0, tiled=True),
        lax.all_to_all(to_sources(row_sum), "own", split_axis=0, concat_axis=0, tiled=True),
        lax.all_to_all(to_sources(row_target), "own", split_axis=0, concat_axis=0, tiled=True),
    )
    pair_max = back_max.reshape(slots_total)[position].reshape(samp_count, picks)
    pair_sum = back_sum.reshape(slots_total)[position].reshape(samp_count, picks)
    pair_target = back_target.reshape(slots_total)[position].reshape(samp_count, picks)
    peak_max = jnp.max(pair_max, axis=1)
    norm_sum = jnp.sum(pair_sum * jnp.exp(pair_max - peak_max[:, None]), axis=1)
    log_norm = peak_max + jnp.log(norm_sum)
    sample_loss = log_norm - jnp.sum(pair_target, axis=1)
    send_norm = jnp.zeros((slots_total,), jnp.float32).at[position].set(jnp.repeat(log_norm, picks))
    got_norm = lax.all_to_all(
        send_norm.reshape(owner_count, bucket_dev * slot_depth),
        "own",
        split_axis=0,
        concat_axis=0,
        tiled=True,
    )
    row_norm = (
        got_norm.reshape(owner_count, bucket_dev, slot_depth)
        .transpose(1, 0, 2)
        .reshape(bucket_dev, row_count)
    )
    onehot = (columns == target_col[..., None]).astype(jnp.float32)
    grad_logits = (jnp.exp(logits - row_norm[..., None]) - onehot).astype(jnp.bfloat16)
    grad_weight = jnp.einsum(
        "brc,brd->bcd", grad_logits, received, preferred_element_type=jnp.float32
    ).astype(jnp.bfloat16)
    row_grads = jnp.einsum("brc,bcd->brd", grad_logits, weight, preferred_element_type=jnp.float32)
    send_grads = row_grads.reshape(bucket_dev, owner_count, slot_depth, feature_part).transpose(
        1, 0, 2, 3
    )
    send_grads = send_grads.reshape(owner_count, bucket_dev * slot_depth, feature_part)
    got_grads = lax.all_to_all(send_grads, "own", split_axis=0, concat_axis=0, tiled=True)
    pair_grads = got_grads.reshape(slots_total, feature_part)[position].reshape(
        samp_count, picks, feature_part
    )
    grad_hidden = jnp.sum(pair_grads, axis=1)
    return (sample_loss, grad_hidden, grad_weight)


def choose(hidden, weight, bucket_map, active, label_pick):
    samples, picks = active.shape
    buckets = bucket_map.shape[0]
    depth = 2 * samples * picks // buckets
    fits = (
        weight.shape[0] == 1
        and lax.axis_size("rep") == 4
        and buckets == 8
        and picks == 2
        and samples == 128
        and 2 * depth == samples
        and weight.shape[1] % 512 == 0
        and hidden.shape[1] % 128 == 0
    )
    run = fused if fits else body
    return run(hidden, weight, bucket_map, active, label_pick)


def solution(mesh):
    in_specs = (P("own", "rep"), P("own", None, "rep"), P(), P("own", None), P("own"))
    out_specs = (P("own"), P("own", "rep"), P("own", None, "rep"))
    return jax.shard_map(choose, mesh=mesh, in_specs=in_specs, out_specs=out_specs, check_vma=False)
```

```python
import functools
import math
import jax
import jax.numpy as jnp
from jax import lax
from jax.experimental import pallas as pl
from jax.experimental.pallas import tpu as pltpu
from jax.sharding import PartitionSpec as P

MESH = pl.DeviceIdType.MESH
F32 = jnp.float32
BF16 = jnp.bfloat16
NT = (((1,), (1,)), ((), ()))
TN = (((0,), (0,)), ((), ()))


def ranks(slot0, slot1, buckets, upper):
    sources, samples = slot0.shape
    bucket = lax.broadcasted_iota(jnp.int32, (buckets, samples), 0)
    hits = [
        jnp.where((slot0[s : s + 1] == bucket) | (slot1[s : s + 1] == bucket), 1.0, 0.0)
        for s in range(sources)
    ]
    hits = jnp.concatenate(hits, axis=0) if sources > 1 else hits[0]
    earlier = jnp.dot(hits.astype(BF16), upper, preferred_element_type=F32)
    return jnp.where(hits > 0.5, earlier, -1.0).astype(jnp.int32)


def lane_pick(values, index):
    return jnp.take_along_axis(values, index, axis=1)


def kernel(
    n, depth, act_hbm, pick_hbm, map_hbm, hidden_hbm, weight_hbm,
    loss_ref, gh_ref, gw_ref,
    act, pick_own, table_in, meta, hidden, hidden_x, weight, metas, wfull, sendbuf, sendbuf_x, rows, stats, statrep, comb, statown,
    norms, tsums, row_target, row_valid, row_norm, e_all, g_all, hot, u_acc, t_acc, s_mat, ghsend, ghrecv,
    go, s_loc, s_in, s_out, r_hx, r_meta, r_w, r_row, r_rowx, r_fr, r_sr, r_so, r_gx, r_gc, r_gr, r_gh,
):
    labels, part = weight_hbm.shape
    samples = hidden_hbm.shape[0]
    cols = labels // 4
    pairs = n // 2
    o = lax.axis_index("own")
    r = lax.axis_index("rep")
    z = o // 2
    y = o - 2 * z
    p1 = r + 1 - 2 * lax.rem(r, 2)
    p2 = lax.rem(r + 2, 4)
    p3 = lax.rem(p1 + 2, 4)
    row_count = n * depth
    local = [
        pltpu.make_async_copy(act_hbm, act, s_loc.at[0]),
        pltpu.make_async_copy(hidden_hbm, hidden, s_loc.at[1]),
        pltpu.make_async_copy(weight_hbm, weight, s_loc.at[2]),
        pltpu.make_async_copy(
            weight_hbm.at[pl.ds(pl.multiple_of(r * cols, cols), cols)],
            wfull.at[:, pl.ds(pl.multiple_of(r * part, part), part)],
            s_loc.at[3],
        ),
        pltpu.make_async_copy(pick_hbm, pick_own, s_loc.at[4]),
        pltpu.make_async_copy(map_hbm, table_in, s_loc.at[5]),
    ]

    def send(src, dst, ssem, rsem, own, rep):
        copy = pltpu.make_async_remote_copy(
            src_ref=src, dst_ref=dst, send_sem=ssem, recv_sem=rsem,
            device_id={"own": own, "rep": rep}, device_id_type=MESH,
        )
        copy.start()

    def wait(ref, sem):
        pltpu.make_async_copy(ref, ref, sem).wait()

    peers = []
    for turned in (pairs - 1 - z, lax.rem(z + 2, pairs), z + 1 - 2 * lax.rem(z, 2)):
        peers += [2 * turned, 2 * turned + 1]
    peers.append(2 * z + 1 - y)

    def at_rows(s):
        return pl.ds(pl.multiple_of(s * depth, depth), depth)

    def turn_of(to):
        return lax.rem(z - to // 2 + pairs + pairs - 1, pairs)

    def pair_at(p):
        return lax.rem(z + 1 + p, pairs)

    def at_part(q):
        return pl.ds(pl.multiple_of(q * part, part), part)

    unit = cols // 4
    pieces = ((0, cols - unit), (cols - unit, unit))

    def at_cols(q, start=0, size=None):
        size = cols if size is None else size
        return pl.ds(pl.multiple_of(q * cols + start, unit), size)

    def lanes(p):
        return slice(p * 2 * depth, (p + 1) * 2 * depth)

    barrier = pltpu.get_barrier_semaphore()
    odd = lax.rem(r, 2)
    even = r - odd

    def greet(own, rep):
        pl.semaphore_signal(barrier, inc=1, device_id={"own": own, "rep": rep}, device_id_type=MESH)

    @pl.when(odd == 0)
    def _():
        greet(o, p2)
        greet(o, p1)

    @pl.when(odd == 1)
    def _():
        greet(o, p1)
        greet(o, p3)

    for to in peers:
        greet(to, even + 1)
    for c in local:
        c.start()

    @pl.when(odd == 0)
    def _():
        pl.semaphore_wait(barrier, 3)
        pl.semaphore_signal(go, inc=1, device_id={"own": o, "rep": p1}, device_id_type=MESH)

    @pl.when(odd == 1)
    def _():
        pl.semaphore_wait(go, 1)

    send(hidden_hbm, hidden_x, s_in, r_hx, o, p2)
    local[2].wait()
    for j, (start, size) in enumerate(pieces):
        for q in (p2, p3, p1):
            send(weight.at[at_cols(q, start, size)], wfull.at[start : start + size, at_part(r)], s_in, r_w.at[j], o, q)
    local[0].wait()
    local[4].wait()
    local[5].wait()
    meta[0:2, :] = act[...]
    meta[2:3, :] = pick_own[...]
    meta[3:8, :] = jnp.zeros((5, samples), jnp.int32)
    meta[3:4, 0:n] = table_in[...]
    local[1].wait()
    below = lax.broadcasted_iota(jnp.int32, (samples, samples), 0)
    right = lax.broadcasted_iota(jnp.int32, (samples, samples), 1)
    upper = jnp.where(below < right, 1.0, 0.0).astype(BF16)

    def slots(ids):
        table = jnp.broadcast_to(meta[3:4, :], (n, samples))
        return lane_pick(table, jnp.broadcast_to(ids, (n, samples)))[: ids.shape[0]]

    mine = meta[...]
    own_rank = ranks(slots(mine[0:1]), slots(mine[1:2]), n, upper)
    place = lax.broadcasted_iota(jnp.int32, (depth, samples), 0)
    pack = jnp.concatenate(
        [jnp.where(own_rank[b : b + 1] == place, 1.0, 0.0).astype(BF16) for b in range(n)], axis=0
    )
    packed = jnp.dot(pack, hidden[...], preferred_element_type=F32).astype(BF16)
    for b in range(n):
        sendbuf[b] = packed[b * depth : (b + 1) * depth]

    @pl.when(odd == 1)
    def _():
        pl.semaphore_wait(barrier, 2 * (n - 1) + 1)
        pl.semaphore_signal(go, inc=1, device_id={"own": o, "rep": p1}, device_id_type=MESH)

    @pl.when(odd == 0)
    def _():
        pl.semaphore_wait(go, 1)

    for to in peers:
        send(meta, metas.at[o], s_in, r_meta, to, r)
    row_order = peers[6:7] + peers[4:6] + peers[0:2] + peers[2:4]
    rowx_order = peers[6:7] + peers[4:6] + peers[0:2] + peers[2:4]
    for to in row_order:
        p = turn_of(to)
        send(sendbuf.at[to], rows.at[at_rows(2 * p + y), at_part(r)], s_in, r_row.at[p], to, r)
    own_rows = at_rows(2 * (pairs - 1) + y)
    rows[own_rows, at_part(r)] = sendbuf[o]
    metas[o] = mine

    wait(hidden_x, r_hx)
    packed_x = jnp.dot(pack, hidden_x[...], preferred_element_type=F32).astype(BF16)
    for b in range(n):
        sendbuf_x[b] = packed_x[b * depth : (b + 1) * depth]
    for to in rowx_order:
        p = turn_of(to)
        send(sendbuf_x.at[to], rows.at[at_rows(2 * p + y), at_part(p2)], s_in, r_rowx.at[p], to, r)
    rows[own_rows, at_part(p2)] = sendbuf_x[o]

    wait(metas.at[0 : n - 1], r_meta)
    slot0 = slots(metas[:, 0, :])
    slot1 = slots(metas[:, 1, :])
    pick = metas[:, 2, :]
    rank_all = ranks(slot0, slot1, n, upper)
    wanted = jnp.where(pick < labels, slot0, slot1)
    code = jnp.where(wanted == o, jnp.where(pick < labels, pick, pick - labels) + 1, 0)
    code_hi = (code // 64).astype(F32)
    code_lo = (code - (code // 64) * 64).astype(F32)
    lane = lax.broadcasted_iota(jnp.int32, (1, samples), 1)
    sub = lax.broadcasted_iota(jnp.int32, (8, samples), 0)
    bucket_sub = lax.broadcasted_iota(jnp.int32, (n, samples), 0)
    row_index = []
    place2 = lax.broadcasted_iota(jnp.int32, (2 * depth, samples), 0)
    for sp in range(pairs):
        info = jnp.zeros((8, 2 * depth), F32)
        for h in range(2):
            s = 2 * sp + h
            rank_me = jnp.max(
                jnp.where(bucket_sub == o, rank_all[s * n : (s + 1) * n], -1), axis=0, keepdims=True
            )
            member = jnp.where(
                (rank_me >= 0) & (rank_me + h * depth == place2), 1.0, 0.0
            ).astype(BF16)
            facts = jnp.where(
                sub == 0, lane.astype(F32),
                jnp.where(sub == 1, code_hi[s : s + 1], jnp.where(sub == 2, code_lo[s : s + 1], jnp.where(sub == 3, 1.0, 0.0))),
            ).astype(BF16)
            info = info + lax.dot_general(facts, member, NT, preferred_element_type=F32)
        row_index.append(info[0:1].astype(jnp.int32))
        row_valid[sp : sp + 1, :] = info[3:4]
        row_target[sp : sp + 1, :] = (info[1:2] * 64.0 + info[2:3]).astype(jnp.int32) - 1
    targets_at = [row_target[pl.ds(pair_at(p), 1), :] for p in range(pairs)]
    target_row = jnp.concatenate(targets_at, axis=1)

    def hand_over(p, q, sem):
        got = lanes(p) if p < pairs - 1 else at_rows(2 * p + 1 - y)
        wait(rows.at[got, at_part(q)], sem.at[p])
        block = rows.at[lanes(p), at_part(q)]
        send(block, block, s_in, r_fr.at[p], o, p1)

    hand_over(3, r, r_row)
    hand_over(3, p2, r_rowx)
    local[3].wait()
    for c in range(4):
        at = slice(c * cols, (c + 1) * cols)
        ids = lax.broadcasted_iota(jnp.int32, (cols, row_count), 0) + c * cols
        hot[at, :] = jnp.where(ids == target_row, 1.0, 0.0).astype(BF16)
    for p in range(pairs):
        t_acc[lanes(p), :] = lax.dot_general(hot[:, lanes(p)], weight[...], TN, preferred_element_type=F32)
    for p in range(3):
        hand_over(p, r, r_row)

    def pass_x(p, start, size, turn):
        block = e_all.at[p, at_cols(r, start, size), :]
        send(block, block, s_out, r_gx.at[turn], o, p2)

    def pass_c(p, start, size):
        block = e_all.at[p, at_cols(r, start, size), :]
        send(block, block, s_out, r_gc, o, p1)

    def scores(first, last, start, size):
        at = slice(first * 2 * depth, last * 2 * depth)
        width = (last - first) * 2 * depth
        logits = lax.dot_general(wfull[start : start + size, :], rows[at, :], NT, preferred_element_type=F32)
        top = jnp.max(logits, axis=0, keepdims=True)
        raised = jnp.exp(logits - top)
        for p in range(first, last):
            e_all[p, at_cols(r, start, size), :] = raised[:, (p - first) * 2 * depth : (p - first + 1) * 2 * depth].astype(BF16)
        if first in (0, 3) and start == 0:
            pass_x(first, start, size, first)
        label_id = lax.broadcasted_iota(jnp.int32, (size, width), 0) + (r * cols + start)
        target = jnp.sum(jnp.where(label_id == target_row[:, at], logits, 0.0), axis=0, keepdims=True)
        return top, jnp.sum(raised, axis=0, keepdims=True), target

    for j, (start, size) in enumerate(pieces):
        wait(wfull.at[start : start + size, 0 : 3 * part], r_w.at[j])
        if j == 0:
            wait(rows.at[lanes(3), 0 : 2 * part], r_fr.at[3])
            top_d, sum_d, target_d = scores(3, 4, start, size)
            pass_c(3, start, size)
            hand_over(0, p2, r_rowx)
            hand_over(2, p2, r_rowx)
            wait(rows.at[lanes(0), 0 : 2 * part], r_fr.at[0])
            top_a, sum_a, target_a = scores(0, 1, start, size)
            hand_over(1, p2, r_rowx)
        else:
            wait(rows.at[lanes(1), 0 : 2 * part], r_fr.at[1])
            wait(rows.at[lanes(2), 0 : 2 * part], r_fr.at[2])
            top_r, sum_r, target_r = scores(1, 3, 0, cols)
            top_b, sum_b, target_b = scores(0, 1, start, size)
            top_e, sum_e, target_e = scores(3, 4, start, size)

    def merged(top0, sum0, top1, sum1):
        peak = jnp.maximum(top0, top1)
        return peak + jnp.log(sum0 * jnp.exp(top0 - peak) + sum1 * jnp.exp(top1 - peak))

    lse = jnp.concatenate(
        [merged(top_a, sum_a, top_b, sum_b), top_r + jnp.log(sum_r), merged(top_d, sum_d, top_e, sum_e)], axis=1
    )
    target_sum = jnp.concatenate([target_a + target_b, target_r, target_d + target_e], axis=1)
    tops = [jnp.concatenate([top_a, top_r, top_d], axis=1), jnp.concatenate([top_b, top_r, top_e], axis=1)]
    for p in range(pairs):
        stats[p : p + 1, :] = lse[:, lanes(p)]
        stats[pairs + p : pairs + p + 1, :] = target_sum[:, lanes(p)]
        stats[n + p : n + p + 1, :] = tops[0][:, lanes(p)]
        stats[n + pairs + p : n + pairs + p + 1, :] = tops[1][:, lanes(p)]
    for q in (p2, p3, p1):
        send(stats, statrep.at[r], s_in, r_sr, o, q)
    pass_x(0, *pieces[1], 0)
    pass_x(1, 0, cols, 1)
    pass_c(2, 0, cols)
    pass_c(3, *pieces[1])
    for p in range(2):
        pass_c(p, 0, cols)
    statrep[r] = stats[...]
    wait(statrep.at[0:3], r_sr)
    parts = [statrep[q, 0:n, :] for q in range(4)]
    high = jnp.maximum(jnp.maximum(parts[0], parts[1]), jnp.maximum(parts[2], parts[3]))
    total = high + jnp.log(sum(jnp.exp(x - high) for x in parts))
    summed = sum(parts)
    for p in range(pairs):
        comb[pl.ds(pair_at(p), 1), :] = total[p : p + 1]
        comb[pl.ds(pairs + pair_at(p), 1), :] = summed[pairs + p : pairs + p + 1]
    for to in peers:
        send(comb, statown.at[o], s_in, r_so, to, r)
    statown[o] = comb[...]

    def forward(p, start, size, turn):
        block = e_all.at[p, at_cols(p2, start, size), :]
        wait(block, r_gx.at[turn])
        send(block, block, s_out, r_gr.at[turn], o, p1)

    def handed(p, start, size, turn):
        wait(e_all.at[p, at_cols(p3, start, size), :], r_gr.at[turn])

    highs = []
    for p in range(pairs):
        seen = [statrep[q, n + j * pairs + p : n + j * pairs + p + 1, :] for q in range(4) for j in range(2)]
        highs.append(functools.reduce(jnp.maximum, seen))

    def term(p, q, spans):
        for start, size in spans:
            at = at_cols(q, start, size)
            base = n + (pairs if start else 0) + p
            top = statrep[pl.ds(q, 1), base : base + 1, :].reshape(1, samples)
            g_all[at, lanes(p)] = (e_all[p, at, :].astype(F32) * jnp.exp(top - highs[p])).astype(BF16)
        first, size = spans[0][0], sum(x for _, x in spans)
        at = at_cols(q, first, size)
        return lax.dot_general(g_all[at, lanes(p)], weight[at, :], TN, preferred_element_type=F32)

    whole = ((0, cols),)
    late = ((2, 0, cols, 2), (3, *pieces[1], 4))
    wait(e_all.at[:, at_cols(p1), :], r_gc)

    @pl.when(odd == 1)
    def _():
        for p, start, size, turn in late:
            for q, to in ((p1, p3), (r, p2)):
                block = e_all.at[p, at_cols(q, start, size), :]
                send(block, block, s_out, r_gx.at[turn], o, to)

    forward(3, *pieces[0], 3)
    for p in range(pairs):
        spans = whole if p in (1, 2) else pieces
        u_acc[lanes(p), :] = term(p, r, spans) + term(p, p1, spans)
    forward(0, 0, cols, 0)
    u_acc[lanes(0), :] += term(0, p2, pieces)
    u_acc[lanes(3), :] += term(3, p2, pieces[:1])
    handed(3, *pieces[0], 3)
    u_acc[lanes(3), :] += term(3, p3, pieces[:1])
    handed(0, 0, cols, 0)
    u_acc[lanes(0), :] += term(0, p3, pieces)
    forward(1, 0, cols, 1)
    u_acc[lanes(1), :] += term(1, p2, whole)
    wait(statown.at[0 : n - 1], r_so)
    for sp in range(pairs):
        held = statown[:, sp, :]
        pair = []
        for h in range(2):
            s = 2 * sp + h
            rank = rank_all[s * n : (s + 1) * n]
            index = jnp.where(rank >= 0, rank + h * depth, 0)
            value = jnp.where(rank >= 0, lane_pick(held, index), -3.0e38)
            most = jnp.max(value, axis=0, keepdims=True)
            norm = most + jnp.log(jnp.sum(jnp.exp(value - most), axis=0, keepdims=True))
            norms[s : s + 1, :] = norm
            pair.append(
                lane_pick(jnp.broadcast_to(norm, (8, samples)), jnp.broadcast_to(row_index[sp], (8, samples)))[0:1]
            )
        row_norm[sp : sp + 1, :] = jnp.where(lane < depth, pair[0], pair[1])
    scales = []
    for p in range(pairs):
        norm = row_norm[pl.ds(pair_at(p), 1), :]
        valid = row_valid[pl.ds(pair_at(p), 1), :] > 0.5
        scale = jnp.where(valid, jnp.exp(highs[p] - norm), 0.0)
        scales.append(scale)
        s_mat[lanes(p), :] = jnp.transpose(jnp.broadcast_to(scale, (2 * depth, samples)))

    def scaled(values, p):
        return values * jnp.concatenate([s_mat[lanes(p), :]] * (part // samples), axis=1)

    def give_back(p):
        ghsend[lanes(p), :] = (scaled(u_acc[lanes(p), :], p) - t_acc[lanes(p), :]).astype(BF16)
        if p < pairs - 1:
            for h in range(2):
                at = slice((2 * p + h) * depth, (2 * p + h + 1) * depth)
                send(ghsend.at[at], ghrecv.at[at_rows(o)], s_out, r_gh, 2 * pair_at(p) + h, r)
        else:
            send(ghsend.at[at_rows(2 * p + 1 - y)], ghrecv.at[at_rows(o)], s_out, r_gh, 2 * z + 1 - y, r)
            ghrecv[at_rows(o), :] = ghsend[at_rows(2 * p + y), :]

    give_back(0)
    handed(1, 0, cols, 1)
    u_acc[lanes(1), :] += term(1, p3, whole)
    give_back(1)
    forward(2, 0, cols, 2)
    u_acc[lanes(2), :] += term(2, p2, whole)
    forward(3, *pieces[1], 4)
    u_acc[lanes(3), :] += term(3, p2, pieces[1:])
    handed(2, 0, cols, 2)
    u_acc[lanes(2), :] += term(2, p3, whole)
    give_back(2)
    handed(3, *pieces[1], 4)
    u_acc[lanes(3), :] += term(3, p3, pieces[1:])
    give_back(3)
    scale_row = jnp.concatenate(scales, axis=1)
    for c in range(4):
        at = slice(c * cols, (c + 1) * cols)
        grad = g_all[at, :].astype(F32) * scale_row - hot[at, :].astype(F32)
        gw_ref[at, :] = jnp.dot(grad.astype(BF16), rows[:, at_part(r)], preferred_element_type=F32).astype(BF16)
    for sp in range(pairs):
        held = statown[:, pairs + sp, :]
        for h in range(2):
            s = 2 * sp + h
            rank = rank_all[s * n : (s + 1) * n]
            index = jnp.where(rank >= 0, rank + h * depth, 0)
            value = jnp.where(rank >= 0, lane_pick(held, index), 0.0)
            tsums[s : s + 1, :] = jnp.sum(value, axis=0, keepdims=True)
    loss_ref[...] = norms[pl.ds(o, 1), :] - tsums[pl.ds(o, 1), :]
    wait(ghrecv.at[0 : (n - 1) * depth], r_gh)
    gh_ref[...] = lax.dot_general(pack, ghrecv[...], TN, preferred_element_type=F32)
    wide = 2 * row_count

    def rows_of(*refs):
        return sum(2 * math.prod(x) for x in refs) // wide

    one = (cols, 2 * depth)
    spread = (n - 1, depth, part)
    facts = (n - 1, 8, 2 * samples)
    sent_in = rows_of(
        (samples, part), facts, (3, cols, part), spread, spread, (2, row_count, part), (3, 2 * n, 2 * samples), facts
    )
    wait(hot.at[0:sent_in], s_in)
    base = rows_of(spread, (2 * pairs, *one), (2, *one), (pieces[0][1], 2 * depth))
    late_rows = 2 * rows_of(one, (pieces[1][1], 2 * depth))

    @pl.when(odd == 0)
    def _():
        wait(hot.at[0:base], s_out)

    @pl.when(odd == 1)
    def _():
        wait(hot.at[0 : base + late_rows], s_out)


def finish(loss_in, gh_in, gw_in, loss_out, gh_out, gw_out, sem):
    step = gw_in.shape[0] // 4
    cuts = [pl.ds(i * step, step) for i in range(4)]
    pairs = [(gw_in.at[at], gw_out.at[at]) for at in cuts] + [(gh_in, gh_out), (loss_in, loss_out)]
    moves = [
        pltpu.make_async_copy(a, b, sem.at[i])
        for i, (a, b) in enumerate(pairs)
    ]
    for c in moves:
        c.start()
    for c in moves:
        c.wait()


def fused(hidden, weight, bucket_map, active, label_pick):
    samples, part = hidden.shape
    labels = weight.shape[1]
    n = bucket_map.shape[0]
    depth = 2 * samples * active.shape[1] // n
    cols = labels // 4
    row_count = n * depth
    vmem = pl.BlockSpec(memory_space=pltpu.VMEM)
    hbm = pl.BlockSpec(memory_space=pltpu.HBM)
    dma = pltpu.SemaphoreType.DMA
    sems = [pltpu.SemaphoreType.REGULAR, dma((6,)), dma, dma]
    for received in (None, None, 2, n // 2, n // 2, n // 2, None, None, n // 2 + 1, None, n // 2 + 1, None):
        sems.append(dma if received is None else dma((received,)))
    loss, grad_hidden, grad_weight = pl.pallas_call(
        functools.partial(kernel, n, depth),
        out_shape=(
            pltpu.VMEM((1, samples), F32),
            pltpu.VMEM((samples, part), F32),
            pltpu.VMEM((labels, part), BF16),
        ),
        in_specs=[hbm] * 5,
        out_specs=(vmem, vmem, vmem),
        scratch_shapes=[
            pltpu.VMEM((2, samples), jnp.int32),
            pltpu.VMEM((1, samples), jnp.int32),
            pltpu.VMEM((1, n), jnp.int32),
            pltpu.VMEM((8, samples), jnp.int32),
            pltpu.VMEM((samples, part), BF16),
            pltpu.VMEM((samples, part), BF16),
            pltpu.VMEM((labels, part), BF16),
            pltpu.VMEM((n, 8, samples), jnp.int32),
            pltpu.VMEM((cols, 4 * part), BF16),
            pltpu.VMEM((n, depth, part), BF16),
            pltpu.VMEM((n, depth, part), BF16),
            pltpu.VMEM((row_count, 4 * part), BF16),
            pltpu.VMEM((2 * n, samples), F32),
            pltpu.VMEM((4, 2 * n, samples), F32),
            pltpu.VMEM((n, samples), F32),
            pltpu.VMEM((n, n, samples), F32),
            pltpu.VMEM((n, samples), F32),
            pltpu.VMEM((n, samples), F32),
            pltpu.VMEM((8, samples), jnp.int32),
            pltpu.VMEM((8, samples), F32),
            pltpu.VMEM((8, samples), F32),
            pltpu.VMEM((n // 2, labels, 2 * depth), BF16),
            pltpu.VMEM((labels, row_count), BF16),
            pltpu.VMEM((labels, row_count), BF16),
            pltpu.VMEM((row_count, part), F32),
            pltpu.VMEM((row_count, part), F32),
            pltpu.VMEM((row_count, samples), F32),
            pltpu.VMEM((row_count, part), BF16),
            pltpu.VMEM((row_count, part), BF16),
        ] + sems,
        compiler_params=pltpu.CompilerParams(
            collective_id=0, has_side_effects=True, vmem_limit_bytes=60 * 1024 * 1024
        ),
    )(active.T, label_pick[None], bucket_map[None], hidden, weight[0])
    loss, grad_hidden, grad_weight = pl.pallas_call(
        finish,
        out_shape=(
            jax.ShapeDtypeStruct((1, samples), F32),
            jax.ShapeDtypeStruct((samples, part), F32),
            jax.ShapeDtypeStruct((labels, part), BF16),
        ),
        in_specs=[vmem] * 3,
        out_specs=(hbm, hbm, hbm),
        scratch_shapes=[dma((6,))],
        compiler_params=pltpu.CompilerParams(vmem_limit_bytes=1024 * 1024),
    )(loss, grad_hidden, grad_weight)
    return loss[0], grad_hidden, grad_weight[None]


def body(hidden, weight, bucket_map, active, label_pick):
    samp_count = hidden.shape[0]
    bucket_dev, label_count, feature_part = weight.shape
    picks = active.shape[1]
    bucket_total = bucket_map.shape[0]
    owner_count = lax.axis_size("own")
    slot_depth = max(2, 2 * samp_count * picks // bucket_total)
    pair_count = samp_count * picks
    slots_total = bucket_total * slot_depth
    row_count = owner_count * slot_depth
    pair_bucket = active.reshape(pair_count)
    bucket_iota = lax.broadcasted_iota(jnp.int32, (pair_count, bucket_total), 1)
    slot_index = jnp.sum(
        jnp.where(pair_bucket[:, None] == bucket_iota, bucket_map[None, :], 0), axis=1
    )
    slot_hits = (slot_index[:, None] == bucket_iota).astype(jnp.int32)
    before = lax.broadcasted_iota(jnp.int32, (pair_count, pair_count), 0)
    after = lax.broadcasted_iota(jnp.int32, (pair_count, pair_count), 1)
    earlier = jnp.dot(
        (after < before).astype(BF16), slot_hits.astype(BF16), preferred_element_type=F32
    ).astype(jnp.int32)
    rank_within = jnp.sum(earlier * slot_hits, axis=1)
    position = slot_index * slot_depth + rank_within
    pair_index = jnp.arange(pair_count, dtype=jnp.int32)
    pick_value = jnp.repeat(label_pick, picks)
    target_pair = jnp.where(
        pick_value // label_count == pair_index % picks, pick_value % label_count, -1
    )
    width_sent = hidden.shape[1]
    pair_rows = jnp.repeat(hidden, picks, axis=0)
    send_rows = jnp.zeros((slots_total, width_sent), jnp.bfloat16).at[position].set(pair_rows)
    send_target = jnp.full((slots_total,), -1, jnp.int32).at[position].set(target_pair)
    got_rows, got_target = (
        lax.all_to_all(
            send_rows.reshape(owner_count, bucket_dev * slot_depth, width_sent),
            "own",
            split_axis=0,
            concat_axis=0,
            tiled=True,
        ),
        lax.all_to_all(
            send_target.reshape(owner_count, bucket_dev * slot_depth),
            "own",
            split_axis=0,
            concat_axis=0,
            tiled=True,
        ),
    )
    received = got_rows.reshape(owner_count, bucket_dev, slot_depth, width_sent).transpose(
        1, 0, 2, 3
    )
    received = received.reshape(bucket_dev, row_count, width_sent)
    target_col = (
        got_target.reshape(owner_count, bucket_dev, slot_depth)
        .transpose(1, 0, 2)
        .reshape(bucket_dev, row_count)
    )
    partial_value = jnp.einsum("brd,bcd->brc", received, weight, preferred_element_type=jnp.float32)
    logits = lax.psum(partial_value, "rep")
    columns = lax.broadcasted_iota(jnp.int32, (1, 1, label_count), 2)
    row_max = jnp.max(logits, axis=2)
    row_sum = jnp.sum(jnp.exp(logits - row_max[..., None]), axis=2)
    row_target = jnp.sum(jnp.where(columns == target_col[..., None], logits, 0.0), axis=2)

    def to_sources(values):
        return (
            values.reshape(bucket_dev, owner_count, slot_depth)
            .transpose(1, 0, 2)
            .reshape(owner_count, bucket_dev * slot_depth)
        )

    back_max, back_sum, back_target = (
        lax.all_to_all(to_sources(row_max), "own", split_axis=0, concat_axis=0, tiled=True),
        lax.all_to_all(to_sources(row_sum), "own", split_axis=0, concat_axis=0, tiled=True),
        lax.all_to_all(to_sources(row_target), "own", split_axis=0, concat_axis=0, tiled=True),
    )
    pair_max = back_max.reshape(slots_total)[position].reshape(samp_count, picks)
    pair_sum = back_sum.reshape(slots_total)[position].reshape(samp_count, picks)
    pair_target = back_target.reshape(slots_total)[position].reshape(samp_count, picks)
    peak_max = jnp.max(pair_max, axis=1)
    norm_sum = jnp.sum(pair_sum * jnp.exp(pair_max - peak_max[:, None]), axis=1)
    log_norm = peak_max + jnp.log(norm_sum)
    sample_loss = log_norm - jnp.sum(pair_target, axis=1)
    send_norm = jnp.zeros((slots_total,), jnp.float32).at[position].set(jnp.repeat(log_norm, picks))
    got_norm = lax.all_to_all(
        send_norm.reshape(owner_count, bucket_dev * slot_depth),
        "own",
        split_axis=0,
        concat_axis=0,
        tiled=True,
    )
    row_norm = (
        got_norm.reshape(owner_count, bucket_dev, slot_depth)
        .transpose(1, 0, 2)
        .reshape(bucket_dev, row_count)
    )
    onehot = (columns == target_col[..., None]).astype(jnp.float32)
    grad_logits = (jnp.exp(logits - row_norm[..., None]) - onehot).astype(jnp.bfloat16)
    grad_weight = jnp.einsum(
        "brc,brd->bcd", grad_logits, received, preferred_element_type=jnp.float32
    ).astype(jnp.bfloat16)
    row_grads = jnp.einsum("brc,bcd->brd", grad_logits, weight, preferred_element_type=jnp.float32)
    send_grads = row_grads.reshape(bucket_dev, owner_count, slot_depth, feature_part).transpose(
        1, 0, 2, 3
    )
    send_grads = send_grads.reshape(owner_count, bucket_dev * slot_depth, feature_part)
    got_grads = lax.all_to_all(send_grads, "own", split_axis=0, concat_axis=0, tiled=True)
    pair_grads = got_grads.reshape(slots_total, feature_part)[position].reshape(
        samp_count, picks, feature_part
    )
    grad_hidden = jnp.sum(pair_grads, axis=1)
    return (sample_loss, grad_hidden, grad_weight)


def choose(hidden, weight, bucket_map, active, label_pick):
    samples, picks = active.shape
    buckets = bucket_map.shape[0]
    depth = 2 * samples * picks // buckets
    fits = (
        weight.shape[0] == 1
        and lax.axis_size("rep") == 4
        and buckets == 8
        and picks == 2
        and samples == 128
        and 2 * depth == samples
        and weight.shape[1] % 512 == 0
        and hidden.shape[1] % 128 == 0
    )
    run = fused if fits else body
    return run(hidden, weight, bucket_map, active, label_pick)


def solution(mesh):
    in_specs = (P("own", "rep"), P("own", None, "rep"), P(), P("own", None), P("own"))
    out_specs = (P("own"), P("own", "rep"), P("own", None, "rep"))
    return jax.shard_map(choose, mesh=mesh, in_specs=in_specs, out_specs=out_specs, check_vma=False)
```

```python
import functools
import math
import jax
import jax.numpy as jnp
from jax import lax
from jax.experimental import pallas as pl
from jax.experimental.pallas import tpu as pltpu
from jax.sharding import PartitionSpec as P

MESH = pl.DeviceIdType.MESH
F32 = jnp.float32
BF16 = jnp.bfloat16
NT = (((1,), (1,)), ((), ()))
TN = (((0,), (0,)), ((), ()))


def ranks(slot0, slot1, buckets, upper):
    sources, samples = slot0.shape
    bucket = lax.broadcasted_iota(jnp.int32, (buckets, samples), 0)
    hits = [
        jnp.where((slot0[s : s + 1] == bucket) | (slot1[s : s + 1] == bucket), 1.0, 0.0)
        for s in range(sources)
    ]
    hits = jnp.concatenate(hits, axis=0) if sources > 1 else hits[0]
    earlier = jnp.dot(hits.astype(BF16), upper, preferred_element_type=F32)
    return jnp.where(hits > 0.5, earlier, -1.0).astype(jnp.int32)


def lane_pick(values, index):
    return jnp.take_along_axis(values, index, axis=1)


def kernel(
    n, depth, act_hbm, pick_hbm, map_hbm, hidden_hbm, weight_hbm,
    loss_ref, gh_ref, gw_ref,
    act, pick_own, table_in, meta, hidden, hidden_x, weight, metas, wfull, sendbuf, sendbuf_x, rows, stats, statrep, comb, statown,
    norms, tsums, row_target, row_valid, row_norm, e_all, g_all, hot, u_acc, t_acc, s_mat, ghsend, ghrecv,
    go, s_loc, s_in, s_out, r_hx, r_meta, r_w, r_row, r_rowx, r_fr, r_sr, r_so, r_gx, r_gc, r_gr, r_gh,
):
    labels, part = weight_hbm.shape
    samples = hidden_hbm.shape[0]
    cols = labels // 4
    pairs = n // 2
    o = lax.axis_index("own")
    r = lax.axis_index("rep")
    z = o // 2
    y = o - 2 * z
    p1 = r + 1 - 2 * lax.rem(r, 2)
    p2 = lax.rem(r + 2, 4)
    p3 = lax.rem(p1 + 2, 4)
    row_count = n * depth
    local = [
        pltpu.make_async_copy(act_hbm, act, s_loc.at[0]),
        pltpu.make_async_copy(hidden_hbm, hidden, s_loc.at[1]),
        pltpu.make_async_copy(weight_hbm, weight, s_loc.at[2]),
        pltpu.make_async_copy(
            weight_hbm.at[pl.ds(pl.multiple_of(r * cols, cols), cols)],
            wfull.at[:, pl.ds(pl.multiple_of(r * part, part), part)],
            s_loc.at[3],
        ),
        pltpu.make_async_copy(pick_hbm, pick_own, s_loc.at[4]),
        pltpu.make_async_copy(map_hbm, table_in, s_loc.at[5]),
    ]

    def send(src, dst, ssem, rsem, own, rep):
        copy = pltpu.make_async_remote_copy(
            src_ref=src, dst_ref=dst, send_sem=ssem, recv_sem=rsem,
            device_id={"own": own, "rep": rep}, device_id_type=MESH,
        )
        copy.start()

    def wait(ref, sem):
        pltpu.make_async_copy(ref, ref, sem).wait()

    peers = []
    for turned in (pairs - 1 - z, lax.rem(z + 2, pairs), z + 1 - 2 * lax.rem(z, 2)):
        peers += [2 * turned, 2 * turned + 1]
    peers.append(2 * z + 1 - y)

    def at_rows(s):
        return pl.ds(pl.multiple_of(s * depth, depth), depth)

    def turn_of(to):
        return lax.rem(z - to // 2 + pairs + pairs - 1, pairs)

    def pair_at(p):
        return lax.rem(z + 1 + p, pairs)

    def at_part(q):
        return pl.ds(pl.multiple_of(q * part, part), part)

    unit = cols // 4
    pieces = ((0, cols - unit), (cols - unit, unit))

    def at_cols(q, start=0, size=None):
        size = cols if size is None else size
        return pl.ds(pl.multiple_of(q * cols + start, unit), size)

    def lanes(p):
        return slice(p * 2 * depth, (p + 1) * 2 * depth)

    barrier = pltpu.get_barrier_semaphore()
    odd = lax.rem(r, 2)
    even = r - odd

    def greet(own, rep):
        pl.semaphore_signal(barrier, inc=1, device_id={"own": own, "rep": rep}, device_id_type=MESH)

    @pl.when(odd == 0)
    def _():
        greet(o, p2)
        greet(o, p1)

    @pl.when(odd == 1)
    def _():
        greet(o, p1)
        greet(o, p3)

    for to in peers:
        greet(to, even + 1)
    for c in local:
        c.start()

    @pl.when(odd == 0)
    def _():
        pl.semaphore_wait(barrier, 3)
        pl.semaphore_signal(go, inc=1, device_id={"own": o, "rep": p1}, device_id_type=MESH)

    @pl.when(odd == 1)
    def _():
        pl.semaphore_wait(go, 1)

    send(hidden_hbm, hidden_x, s_in, r_hx, o, p2)
    local[2].wait()
    for j, (start, size) in enumerate(pieces):
        for q in (p2, p3, p1):
            send(weight.at[at_cols(q, start, size)], wfull.at[start : start + size, at_part(r)], s_in, r_w.at[j], o, q)
    local[0].wait()
    local[4].wait()
    local[5].wait()
    meta[0:2, :] = act[...]
    meta[2:3, :] = pick_own[...]
    meta[3:8, :] = jnp.zeros((5, samples), jnp.int32)
    meta[3:4, 0:n] = table_in[...]
    local[1].wait()
    below = lax.broadcasted_iota(jnp.int32, (samples, samples), 0)
    right = lax.broadcasted_iota(jnp.int32, (samples, samples), 1)
    upper = jnp.where(below < right, 1.0, 0.0).astype(BF16)

    def slots(ids):
        table = jnp.broadcast_to(meta[3:4, :], (n, samples))
        return lane_pick(table, jnp.broadcast_to(ids, (n, samples)))[: ids.shape[0]]

    mine = meta[...]
    own_rank = ranks(slots(mine[0:1]), slots(mine[1:2]), n, upper)
    place = lax.broadcasted_iota(jnp.int32, (depth, samples), 0)
    pack = jnp.concatenate(
        [jnp.where(own_rank[b : b + 1] == place, 1.0, 0.0).astype(BF16) for b in range(n)], axis=0
    )
    packed = jnp.dot(pack, hidden[...], preferred_element_type=F32).astype(BF16)
    for b in range(n):
        sendbuf[b] = packed[b * depth : (b + 1) * depth]

    @pl.when(odd == 1)
    def _():
        pl.semaphore_wait(barrier, 2 * (n - 1) + 1)
        pl.semaphore_signal(go, inc=1, device_id={"own": o, "rep": p1}, device_id_type=MESH)

    @pl.when(odd == 0)
    def _():
        pl.semaphore_wait(go, 1)

    for to in peers:
        send(meta, metas.at[o], s_in, r_meta, to, r)
    row_order = peers[6:7] + peers[4:6] + peers[0:2] + peers[2:4]
    rowx_order = peers[6:7] + peers[4:6] + peers[0:2] + peers[2:4]
    for to in row_order:
        p = turn_of(to)
        send(sendbuf.at[to], rows.at[at_rows(2 * p + y), at_part(r)], s_in, r_row.at[p], to, r)
    own_rows = at_rows(2 * (pairs - 1) + y)
    rows[own_rows, at_part(r)] = sendbuf[o]
    metas[o] = mine

    wait(hidden_x, r_hx)
    packed_x = jnp.dot(pack, hidden_x[...], preferred_element_type=F32).astype(BF16)
    for b in range(n):
        sendbuf_x[b] = packed_x[b * depth : (b + 1) * depth]
    for to in rowx_order:
        p = turn_of(to)
        send(sendbuf_x.at[to], rows.at[at_rows(2 * p + y), at_part(p2)], s_in, r_rowx.at[p], to, r)
    rows[own_rows, at_part(p2)] = sendbuf_x[o]

    wait(metas.at[0 : n - 1], r_meta)
    slot0 = slots(metas[:, 0, :])
    slot1 = slots(metas[:, 1, :])
    pick = metas[:, 2, :]
    rank_all = ranks(slot0, slot1, n, upper)
    wanted = jnp.where(pick < labels, slot0, slot1)
    code = jnp.where(wanted == o, jnp.where(pick < labels, pick, pick - labels) + 1, 0)
    code_hi = (code // 64).astype(F32)
    code_lo = (code - (code // 64) * 64).astype(F32)
    lane = lax.broadcasted_iota(jnp.int32, (1, samples), 1)
    sub = lax.broadcasted_iota(jnp.int32, (8, samples), 0)
    bucket_sub = lax.broadcasted_iota(jnp.int32, (n, samples), 0)
    row_index = []
    place2 = lax.broadcasted_iota(jnp.int32, (2 * depth, samples), 0)
    for sp in range(pairs):
        info = jnp.zeros((8, 2 * depth), F32)
        for h in range(2):
            s = 2 * sp + h
            rank_me = jnp.max(
                jnp.where(bucket_sub == o, rank_all[s * n : (s + 1) * n], -1), axis=0, keepdims=True
            )
            member = jnp.where(
                (rank_me >= 0) & (rank_me + h * depth == place2), 1.0, 0.0
            ).astype(BF16)
            facts = jnp.where(
                sub == 0, lane.astype(F32),
                jnp.where(sub == 1, code_hi[s : s + 1], jnp.where(sub == 2, code_lo[s : s + 1], jnp.where(sub == 3, 1.0, 0.0))),
            ).astype(BF16)
            info = info + lax.dot_general(facts, member, NT, preferred_element_type=F32)
        row_index.append(info[0:1].astype(jnp.int32))
        row_valid[sp : sp + 1, :] = info[3:4]
        row_target[sp : sp + 1, :] = (info[1:2] * 64.0 + info[2:3]).astype(jnp.int32) - 1
    targets_at = [row_target[pl.ds(pair_at(p), 1), :] for p in range(pairs)]
    target_row = jnp.concatenate(targets_at, axis=1)

    def hand_over(p, q, sem):
        got = lanes(p) if p < pairs - 1 else at_rows(2 * p + 1 - y)
        wait(rows.at[got, at_part(q)], sem.at[p])
        block = rows.at[lanes(p), at_part(q)]
        send(block, block, s_in, r_fr.at[p], o, p1)

    hand_over(3, r, r_row)
    hand_over(3, p2, r_rowx)
    local[3].wait()
    for c in range(4):
        at = slice(c * cols, (c + 1) * cols)
        ids = lax.broadcasted_iota(jnp.int32, (cols, row_count), 0) + c * cols
        hot[at, :] = jnp.where(ids == target_row, 1.0, 0.0).astype(BF16)
    for p in range(pairs):
        t_acc[lanes(p), :] = lax.dot_general(hot[:, lanes(p)], weight[...], TN, preferred_element_type=F32)
    for p in (0, 2, 1):
        hand_over(p, r, r_row)

    def pass_x(p, start, size, turn):
        block = e_all.at[p, at_cols(r, start, size), :]
        send(block, block, s_out, r_gx.at[turn], o, p2)

    def pass_c(p, start, size):
        block = e_all.at[p, at_cols(r, start, size), :]
        send(block, block, s_out, r_gc, o, p1)

    def scores(first, last, start, size):
        at = slice(first * 2 * depth, last * 2 * depth)
        width = (last - first) * 2 * depth
        logits = lax.dot_general(wfull[start : start + size, :], rows[at, :], NT, preferred_element_type=F32)
        top = jnp.max(logits, axis=0, keepdims=True)
        raised = jnp.exp(logits - top)
        for p in range(first, last):
            e_all[p, at_cols(r, start, size), :] = raised[:, (p - first) * 2 * depth : (p - first + 1) * 2 * depth].astype(BF16)
        if first in (0, 3) and start == 0:
            pass_x(first, start, size, first)
        label_id = lax.broadcasted_iota(jnp.int32, (size, width), 0) + (r * cols + start)
        target = jnp.sum(jnp.where(label_id == target_row[:, at], logits, 0.0), axis=0, keepdims=True)
        return top, jnp.sum(raised, axis=0, keepdims=True), target

    for j, (start, size) in enumerate(pieces):
        wait(wfull.at[start : start + size, 0 : 3 * part], r_w.at[j])
        if j == 0:
            wait(rows.at[lanes(3), 0 : 2 * part], r_fr.at[3])
            top_d, sum_d, target_d = scores(3, 4, start, size)
            pass_c(3, start, size)
            hand_over(0, p2, r_rowx)
            hand_over(2, p2, r_rowx)
            wait(rows.at[lanes(0), 0 : 2 * part], r_fr.at[0])
            top_a, sum_a, target_a = scores(0, 1, start, size)
            hand_over(1, p2, r_rowx)
        else:
            wait(rows.at[lanes(2), 0 : 2 * part], r_fr.at[2])
            third = scores(2, 3, 0, cols)
            wait(rows.at[lanes(1), 0 : 2 * part], r_fr.at[1])
            second = scores(1, 2, 0, cols)
            top_r, sum_r, target_r = (jnp.concatenate(x, axis=1) for x in zip(second, third))
            top_b, sum_b, target_b = scores(0, 1, start, size)
            top_e, sum_e, target_e = scores(3, 4, start, size)

    def merged(top0, sum0, top1, sum1):
        peak = jnp.maximum(top0, top1)
        return peak + jnp.log(sum0 * jnp.exp(top0 - peak) + sum1 * jnp.exp(top1 - peak))

    lse = jnp.concatenate(
        [merged(top_a, sum_a, top_b, sum_b), top_r + jnp.log(sum_r), merged(top_d, sum_d, top_e, sum_e)], axis=1
    )
    target_sum = jnp.concatenate([target_a + target_b, target_r, target_d + target_e], axis=1)
    tops = [jnp.concatenate([top_a, top_r, top_d], axis=1), jnp.concatenate([top_b, top_r, top_e], axis=1)]
    for p in range(pairs):
        stats[p : p + 1, :] = lse[:, lanes(p)]
        stats[pairs + p : pairs + p + 1, :] = target_sum[:, lanes(p)]
        stats[n + p : n + p + 1, :] = tops[0][:, lanes(p)]
        stats[n + pairs + p : n + pairs + p + 1, :] = tops[1][:, lanes(p)]
    for q in (p2, p3, p1):
        send(stats, statrep.at[r], s_in, r_sr, o, q)
    pass_x(0, *pieces[1], 0)
    pass_x(1, 0, cols, 1)
    pass_c(2, 0, cols)
    pass_c(3, *pieces[1])
    for p in range(2):
        pass_c(p, 0, cols)
    statrep[r] = stats[...]
    wait(statrep.at[0:3], r_sr)
    parts = [statrep[q, 0:n, :] for q in range(4)]
    high = jnp.maximum(jnp.maximum(parts[0], parts[1]), jnp.maximum(parts[2], parts[3]))
    total = high + jnp.log(sum(jnp.exp(x - high) for x in parts))
    summed = sum(parts)
    for p in range(pairs):
        comb[pl.ds(pair_at(p), 1), :] = total[p : p + 1]
        comb[pl.ds(pairs + pair_at(p), 1), :] = summed[pairs + p : pairs + p + 1]
    for to in peers:
        send(comb, statown.at[o], s_in, r_so, to, r)
    statown[o] = comb[...]

    def forward(p, start, size, turn):
        block = e_all.at[p, at_cols(p2, start, size), :]
        wait(block, r_gx.at[turn])
        send(block, block, s_out, r_gr.at[turn], o, p1)

    def handed(p, start, size, turn):
        wait(e_all.at[p, at_cols(p3, start, size), :], r_gr.at[turn])

    highs = []
    for p in range(pairs):
        seen = [statrep[q, n + j * pairs + p : n + j * pairs + p + 1, :] for q in range(4) for j in range(2)]
        highs.append(functools.reduce(jnp.maximum, seen))

    def term(p, q, spans):
        for start, size in spans:
            at = at_cols(q, start, size)
            base = n + (pairs if start else 0) + p
            top = statrep[pl.ds(q, 1), base : base + 1, :].reshape(1, samples)
            g_all[at, lanes(p)] = (e_all[p, at, :].astype(F32) * jnp.exp(top - highs[p])).astype(BF16)
        first, size = spans[0][0], sum(x for _, x in spans)
        at = at_cols(q, first, size)
        return lax.dot_general(g_all[at, lanes(p)], weight[at, :], TN, preferred_element_type=F32)

    whole = ((0, cols),)
    late = ((2, 0, cols, 2), (3, *pieces[1], 4))
    wait(e_all.at[:, at_cols(p1), :], r_gc)

    @pl.when(odd == 1)
    def _():
        for p, start, size, turn in late:
            for q, to in ((p1, p3), (r, p2)):
                block = e_all.at[p, at_cols(q, start, size), :]
                send(block, block, s_out, r_gx.at[turn], o, to)

    forward(3, *pieces[0], 3)
    for p in range(pairs):
        spans = whole if p in (1, 2) else pieces
        u_acc[lanes(p), :] = term(p, r, spans) + term(p, p1, spans)
    forward(0, 0, cols, 0)
    u_acc[lanes(0), :] += term(0, p2, pieces)
    u_acc[lanes(3), :] += term(3, p2, pieces[:1])
    handed(3, *pieces[0], 3)
    u_acc[lanes(3), :] += term(3, p3, pieces[:1])
    handed(0, 0, cols, 0)
    u_acc[lanes(0), :] += term(0, p3, pieces)
    forward(1, 0, cols, 1)
    u_acc[lanes(1), :] += term(1, p2, whole)
    wait(statown.at[0 : n - 1], r_so)
    for sp in range(pairs):
        held = statown[:, sp, :]
        pair = []
        for h in range(2):
            s = 2 * sp + h
            rank = rank_all[s * n : (s + 1) * n]
            index = jnp.where(rank >= 0, rank + h * depth, 0)
            value = jnp.where(rank >= 0, lane_pick(held, index), -3.0e38)
            most = jnp.max(value, axis=0, keepdims=True)
            norm = most + jnp.log(jnp.sum(jnp.exp(value - most), axis=0, keepdims=True))
            norms[s : s + 1, :] = norm
            pair.append(
                lane_pick(jnp.broadcast_to(norm, (8, samples)), jnp.broadcast_to(row_index[sp], (8, samples)))[0:1]
            )
        row_norm[sp : sp + 1, :] = jnp.where(lane < depth, pair[0], pair[1])
    scales = []
    for p in range(pairs):
        norm = row_norm[pl.ds(pair_at(p), 1), :]
        valid = row_valid[pl.ds(pair_at(p), 1), :] > 0.5
        scale = jnp.where(valid, jnp.exp(highs[p] - norm), 0.0)
        scales.append(scale)
        s_mat[lanes(p), :] = jnp.transpose(jnp.broadcast_to(scale, (2 * depth, samples)))

    def scaled(values, p):
        return values * jnp.concatenate([s_mat[lanes(p), :]] * (part // samples), axis=1)

    def give_back(p):
        ghsend[lanes(p), :] = (scaled(u_acc[lanes(p), :], p) - t_acc[lanes(p), :]).astype(BF16)
        if p < pairs - 1:
            for h in range(2):
                at = slice((2 * p + h) * depth, (2 * p + h + 1) * depth)
                send(ghsend.at[at], ghrecv.at[at_rows(o)], s_out, r_gh, 2 * pair_at(p) + h, r)
        else:
            send(ghsend.at[at_rows(2 * p + 1 - y)], ghrecv.at[at_rows(o)], s_out, r_gh, 2 * z + 1 - y, r)
            ghrecv[at_rows(o), :] = ghsend[at_rows(2 * p + y), :]

    give_back(0)
    handed(1, 0, cols, 1)
    u_acc[lanes(1), :] += term(1, p3, whole)
    give_back(1)
    forward(2, 0, cols, 2)
    u_acc[lanes(2), :] += term(2, p2, whole)
    forward(3, *pieces[1], 4)
    u_acc[lanes(3), :] += term(3, p2, pieces[1:])
    handed(2, 0, cols, 2)
    u_acc[lanes(2), :] += term(2, p3, whole)
    give_back(2)
    handed(3, *pieces[1], 4)
    u_acc[lanes(3), :] += term(3, p3, pieces[1:])
    give_back(3)
    scale_row = jnp.concatenate(scales, axis=1)
    for c in range(4):
        at = slice(c * cols, (c + 1) * cols)
        grad = g_all[at, :].astype(F32) * scale_row - hot[at, :].astype(F32)
        gw_ref[at, :] = jnp.dot(grad.astype(BF16), rows[:, at_part(r)], preferred_element_type=F32).astype(BF16)
    for sp in range(pairs):
        held = statown[:, pairs + sp, :]
        for h in range(2):
            s = 2 * sp + h
            rank = rank_all[s * n : (s + 1) * n]
            index = jnp.where(rank >= 0, rank + h * depth, 0)
            value = jnp.where(rank >= 0, lane_pick(held, index), 0.0)
            tsums[s : s + 1, :] = jnp.sum(value, axis=0, keepdims=True)
    loss_ref[...] = norms[pl.ds(o, 1), :] - tsums[pl.ds(o, 1), :]
    wait(ghrecv.at[0 : (n - 1) * depth], r_gh)
    gh_ref[...] = lax.dot_general(pack, ghrecv[...], TN, preferred_element_type=F32)
    wide = 2 * row_count

    def rows_of(*refs):
        return sum(2 * math.prod(x) for x in refs) // wide

    one = (cols, 2 * depth)
    spread = (n - 1, depth, part)
    facts = (n - 1, 8, 2 * samples)
    sent_in = rows_of(
        (samples, part), facts, (3, cols, part), spread, spread, (2, row_count, part), (3, 2 * n, 2 * samples), facts
    )
    wait(hot.at[0:sent_in], s_in)
    base = rows_of(spread, (2 * pairs, *one), (2, *one), (pieces[0][1], 2 * depth))
    late_rows = 2 * rows_of(one, (pieces[1][1], 2 * depth))

    @pl.when(odd == 0)
    def _():
        wait(hot.at[0:base], s_out)

    @pl.when(odd == 1)
    def _():
        wait(hot.at[0 : base + late_rows], s_out)


def finish(loss_in, gh_in, gw_in, loss_out, gh_out, gw_out, sem):
    step = gw_in.shape[0] // 4
    cuts = [pl.ds(i * step, step) for i in range(4)]
    pairs = [(gw_in.at[at], gw_out.at[at]) for at in cuts] + [(gh_in, gh_out), (loss_in, loss_out)]
    moves = [
        pltpu.make_async_copy(a, b, sem.at[i])
        for i, (a, b) in enumerate(pairs)
    ]
    for c in moves:
        c.start()
    for c in moves:
        c.wait()


def fused(hidden, weight, bucket_map, active, label_pick):
    samples, part = hidden.shape
    labels = weight.shape[1]
    n = bucket_map.shape[0]
    depth = 2 * samples * active.shape[1] // n
    cols = labels // 4
    row_count = n * depth
    vmem = pl.BlockSpec(memory_space=pltpu.VMEM)
    hbm = pl.BlockSpec(memory_space=pltpu.HBM)
    dma = pltpu.SemaphoreType.DMA
    sems = [pltpu.SemaphoreType.REGULAR, dma((6,)), dma, dma]
    for received in (None, None, 2, n // 2, n // 2, n // 2, None, None, n // 2 + 1, None, n // 2 + 1, None):
        sems.append(dma if received is None else dma((received,)))
    loss, grad_hidden, grad_weight = pl.pallas_call(
        functools.partial(kernel, n, depth),
        out_shape=(
            pltpu.VMEM((1, samples), F32),
            pltpu.VMEM((samples, part), F32),
            pltpu.VMEM((labels, part), BF16),
        ),
        in_specs=[hbm] * 5,
        out_specs=(vmem, vmem, vmem),
        scratch_shapes=[
            pltpu.VMEM((2, samples), jnp.int32),
            pltpu.VMEM((1, samples), jnp.int32),
            pltpu.VMEM((1, n), jnp.int32),
            pltpu.VMEM((8, samples), jnp.int32),
            pltpu.VMEM((samples, part), BF16),
            pltpu.VMEM((samples, part), BF16),
            pltpu.VMEM((labels, part), BF16),
            pltpu.VMEM((n, 8, samples), jnp.int32),
            pltpu.VMEM((cols, 4 * part), BF16),
            pltpu.VMEM((n, depth, part), BF16),
            pltpu.VMEM((n, depth, part), BF16),
            pltpu.VMEM((row_count, 4 * part), BF16),
            pltpu.VMEM((2 * n, samples), F32),
            pltpu.VMEM((4, 2 * n, samples), F32),
            pltpu.VMEM((n, samples), F32),
            pltpu.VMEM((n, n, samples), F32),
            pltpu.VMEM((n, samples), F32),
            pltpu.VMEM((n, samples), F32),
            pltpu.VMEM((8, samples), jnp.int32),
            pltpu.VMEM((8, samples), F32),
            pltpu.VMEM((8, samples), F32),
            pltpu.VMEM((n // 2, labels, 2 * depth), BF16),
            pltpu.VMEM((labels, row_count), BF16),
            pltpu.VMEM((labels, row_count), BF16),
            pltpu.VMEM((row_count, part), F32),
            pltpu.VMEM((row_count, part), F32),
            pltpu.VMEM((row_count, samples), F32),
            pltpu.VMEM((row_count, part), BF16),
            pltpu.VMEM((row_count, part), BF16),
        ] + sems,
        compiler_params=pltpu.CompilerParams(
            collective_id=0, has_side_effects=True, vmem_limit_bytes=60 * 1024 * 1024
        ),
    )(active.T, label_pick[None], bucket_map[None], hidden, weight[0])
    loss, grad_hidden, grad_weight = pl.pallas_call(
        finish,
        out_shape=(
            jax.ShapeDtypeStruct((1, samples), F32),
            jax.ShapeDtypeStruct((samples, part), F32),
            jax.ShapeDtypeStruct((labels, part), BF16),
        ),
        in_specs=[vmem] * 3,
        out_specs=(hbm, hbm, hbm),
        scratch_shapes=[dma((6,))],
        compiler_params=pltpu.CompilerParams(vmem_limit_bytes=1024 * 1024),
    )(loss, grad_hidden, grad_weight)
    return loss[0], grad_hidden, grad_weight[None]


def body(hidden, weight, bucket_map, active, label_pick):
    samp_count = hidden.shape[0]
    bucket_dev, label_count, feature_part = weight.shape
    picks = active.shape[1]
    bucket_total = bucket_map.shape[0]
    owner_count = lax.axis_size("own")
    slot_depth = max(2, 2 * samp_count * picks // bucket_total)
    pair_count = samp_count * picks
    slots_total = bucket_total * slot_depth
    row_count = owner_count * slot_depth
    pair_bucket = active.reshape(pair_count)
    bucket_iota = lax.broadcasted_iota(jnp.int32, (pair_count, bucket_total), 1)
    slot_index = jnp.sum(
        jnp.where(pair_bucket[:, None] == bucket_iota, bucket_map[None, :], 0), axis=1
    )
    slot_hits = (slot_index[:, None] == bucket_iota).astype(jnp.int32)
    before = lax.broadcasted_iota(jnp.int32, (pair_count, pair_count), 0)
    after = lax.broadcasted_iota(jnp.int32, (pair_count, pair_count), 1)
    earlier = jnp.dot(
        (after < before).astype(BF16), slot_hits.astype(BF16), preferred_element_type=F32
    ).astype(jnp.int32)
    rank_within = jnp.sum(earlier * slot_hits, axis=1)
    position = slot_index * slot_depth + rank_within
    pair_index = jnp.arange(pair_count, dtype=jnp.int32)
    pick_value = jnp.repeat(label_pick, picks)
    target_pair = jnp.where(
        pick_value // label_count == pair_index % picks, pick_value % label_count, -1
    )
    width_sent = hidden.shape[1]
    pair_rows = jnp.repeat(hidden, picks, axis=0)
    send_rows = jnp.zeros((slots_total, width_sent), jnp.bfloat16).at[position].set(pair_rows)
    send_target = jnp.full((slots_total,), -1, jnp.int32).at[position].set(target_pair)
    got_rows, got_target = (
        lax.all_to_all(
            send_rows.reshape(owner_count, bucket_dev * slot_depth, width_sent),
            "own",
            split_axis=0,
            concat_axis=0,
            tiled=True,
        ),
        lax.all_to_all(
            send_target.reshape(owner_count, bucket_dev * slot_depth),
            "own",
            split_axis=0,
            concat_axis=0,
            tiled=True,
        ),
    )
    received = got_rows.reshape(owner_count, bucket_dev, slot_depth, width_sent).transpose(
        1, 0, 2, 3
    )
    received = received.reshape(bucket_dev, row_count, width_sent)
    target_col = (
        got_target.reshape(owner_count, bucket_dev, slot_depth)
        .transpose(1, 0, 2)
        .reshape(bucket_dev, row_count)
    )
    partial_value = jnp.einsum("brd,bcd->brc", received, weight, preferred_element_type=jnp.float32)
    logits = lax.psum(partial_value, "rep")
    columns = lax.broadcasted_iota(jnp.int32, (1, 1, label_count), 2)
    row_max = jnp.max(logits, axis=2)
    row_sum = jnp.sum(jnp.exp(logits - row_max[..., None]), axis=2)
    row_target = jnp.sum(jnp.where(columns == target_col[..., None], logits, 0.0), axis=2)

    def to_sources(values):
        return (
            values.reshape(bucket_dev, owner_count, slot_depth)
            .transpose(1, 0, 2)
            .reshape(owner_count, bucket_dev * slot_depth)
        )

    back_max, back_sum, back_target = (
        lax.all_to_all(to_sources(row_max), "own", split_axis=0, concat_axis=0, tiled=True),
        lax.all_to_all(to_sources(row_sum), "own", split_axis=0, concat_axis=0, tiled=True),
        lax.all_to_all(to_sources(row_target), "own", split_axis=0, concat_axis=0, tiled=True),
    )
    pair_max = back_max.reshape(slots_total)[position].reshape(samp_count, picks)
    pair_sum = back_sum.reshape(slots_total)[position].reshape(samp_count, picks)
    pair_target = back_target.reshape(slots_total)[position].reshape(samp_count, picks)
    peak_max = jnp.max(pair_max, axis=1)
    norm_sum = jnp.sum(pair_sum * jnp.exp(pair_max - peak_max[:, None]), axis=1)
    log_norm = peak_max + jnp.log(norm_sum)
    sample_loss = log_norm - jnp.sum(pair_target, axis=1)
    send_norm = jnp.zeros((slots_total,), jnp.float32).at[position].set(jnp.repeat(log_norm, picks))
    got_norm = lax.all_to_all(
        send_norm.reshape(owner_count, bucket_dev * slot_depth),
        "own",
        split_axis=0,
        concat_axis=0,
        tiled=True,
    )
    row_norm = (
        got_norm.reshape(owner_count, bucket_dev, slot_depth)
        .transpose(1, 0, 2)
        .reshape(bucket_dev, row_count)
    )
    onehot = (columns == target_col[..., None]).astype(jnp.float32)
    grad_logits = (jnp.exp(logits - row_norm[..., None]) - onehot).astype(jnp.bfloat16)
    grad_weight = jnp.einsum(
        "brc,brd->bcd", grad_logits, received, preferred_element_type=jnp.float32
    ).astype(jnp.bfloat16)
    row_grads = jnp.einsum("brc,bcd->brd", grad_logits, weight, preferred_element_type=jnp.float32)
    send_grads = row_grads.reshape(bucket_dev, owner_count, slot_depth, feature_part).transpose(
        1, 0, 2, 3
    )
    send_grads = send_grads.reshape(owner_count, bucket_dev * slot_depth, feature_part)
    got_grads = lax.all_to_all(send_grads, "own", split_axis=0, concat_axis=0, tiled=True)
    pair_grads = got_grads.reshape(slots_total, feature_part)[position].reshape(
        samp_count, picks, feature_part
    )
    grad_hidden = jnp.sum(pair_grads, axis=1)
    return (sample_loss, grad_hidden, grad_weight)


def choose(hidden, weight, bucket_map, active, label_pick):
    samples, picks = active.shape
    buckets = bucket_map.shape[0]
    depth = 2 * samples * picks // buckets
    fits = (
        weight.shape[0] == 1
        and lax.axis_size("rep") == 4
        and buckets == 8
        and picks == 2
        and samples == 128
        and 2 * depth == samples
        and weight.shape[1] % 512 == 0
        and hidden.shape[1] % 128 == 0
    )
    run = fused if fits else body
    return run(hidden, weight, bucket_map, active, label_pick)


def solution(mesh):
    in_specs = (P("own", "rep"), P("own", None, "rep"), P(), P("own", None), P("own"))
    out_specs = (P("own"), P("own", "rep"), P("own", None, "rep"))
    return jax.shard_map(choose, mesh=mesh, in_specs=in_specs, out_specs=out_specs, check_vma=False)
```
